128 devices in a mesh: loop: 8 (over x_lo, y), grp: 16 (over z, x_hi, core).
Axes of the slice: x: 4 (x_hi: 2, x_lo: 2; x = x_hi * 2 + x_lo), y: 4, z: 4, core: 2. Of those that a mesh axis runs over, the one named last changes fastest.
Arguments:
- queries: bfloat16 [16384, 4096], P(('loop', 'grp')), as said below
- passages: bfloat16 [8192, 4096], P(('loop', 'grp')), as said below
- pool: bfloat16 [32768, 4096], P(('loop', 'grp')), as said below
- query_count: int32 [8, 16], P('loop', 'grp'), may hold values from 32 to 128, as said below
- positive: int32 [16384], P(('loop', 'grp')), may hold values from 0 to 511
- neg_owner: int32 [16384, 7], P(('loop', 'grp')), may hold values from 0 to 15, as said below
- neg_row: int32 [16384, 7], P(('loop', 'grp')), may hold values from 0 to 255
Outputs:
- loss: float32 [16384], P(('loop', 'grp'))
- grad_query: float32 [16384, 4096], P(('loop', 'grp'))
- grad_passage: float32 [8192, 4096], P(('loop', 'grp'))
- grad_pool: float32 [32768, 4096], P(('loop', 'grp'))
The draws below stay inside these ranges and needn't reach their ends.
Inputs may be any that keep to these rules, and one draw needn't show every extreme that they name: `queries`: every entry lies in -0.25 to 0.25. `passages`: every entry lies in -0.25 to 0.25. `pool`: every entry lies in -0.25 to 0.25. `query_count`: some device has all 128 slots live. `neg_owner`: among the 896 entries of one device, at most 70 name one owner; for every loop index one owner is named exactly 70 times by every device of that loop index. Entries of slots that are not live are present too.
All inputs are finite; a program needn't handle non-finite values.
Results may differ from the reference program's by a relative error of at most 0.02.
Values may be sent and summed in bfloat16 or wider, within the bound.
No kernel may reach another device: no remote copies, remote signals or barrier semaphores. Data moves between devices by JAX's collectives and lax.ppermute only.
A program may use at most 192 MiB of HBM per device.

```python
import jax
import jax.numpy as jnp
from jax import lax

D = 4096
Q_DEV = 128
P_DEV = 64
HN = 7
CAP = 70
POOL_DEV = 256
QUERIES = 16384
PASSAGES = 8192
POOL = 32768
N_LOOP = 8
N_GRP = 16


positive_share = 0.13


negative_share = 0.08


noise_share = 0.3


def topic_total():
    return min(32, POOL_DEV)


def topic_table(key):
    return jax.random.normal(jax.random.fold_in(key, 77), (topic_total(), D), jnp.float32)


def passage_topics(key):
    return jax.random.randint(jax.random.fold_in(key, 11), (PASSAGES,), 0, topic_total()).astype(jnp.int32)


def pool_layout(key):
    block_total = N_LOOP * N_GRP
    block_keys = jax.random.split(jax.random.fold_in(key, 12), block_total)

    def one_layout(single_key):
        return jax.random.permutation(single_key, POOL_DEV).astype(jnp.int32)
    return jax.vmap(one_layout)(block_keys)


def pool_topics(key):
    layout = pool_layout(key)
    labels = (jnp.arange(POOL_DEV, dtype=jnp.int32) % topic_total()).astype(jnp.int32)

    def one_block(placed):
        return jnp.zeros((POOL_DEV,), jnp.int32).at[placed].set(labels)
    return jax.vmap(one_block)(layout).reshape(POOL)


def positive_table(key):
    return jax.random.randint(jax.random.fold_in(key, 13), (QUERIES,), 0, N_LOOP * P_DEV).astype(jnp.int32)


def query_blocks():
    block_index = jnp.arange(QUERIES, dtype=jnp.int32) // Q_DEV
    return (block_index // N_GRP, block_index % N_GRP)


def query_topics(key):
    chosen = positive_table(key)
    loop_index, group_index = query_blocks()
    source = (chosen // P_DEV * N_GRP + group_index) * P_DEV + chosen % P_DEV
    return (passage_topics(key)[source], source)


def owner_table(key):
    slot_total = Q_DEV * HN
    tickets = N_GRP * CAP
    busiest = jax.random.randint(jax.random.fold_in(key, 9), (N_LOOP,), 0, N_GRP)

    def one_device(device):
        first, second = jax.random.split(jax.random.fold_in(key, 100 + device))
        labels = (jnp.arange(tickets) // CAP + busiest[device // N_GRP]) % N_GRP
        others = CAP + jax.random.permutation(first, tickets - CAP)
        picked = jnp.concatenate([jnp.arange(CAP), others[:slot_total - CAP]])
        shuffle = jax.random.permutation(second, slot_total)
        return labels[picked][shuffle].reshape(Q_DEV, HN)
    owners = jax.vmap(one_device)(jnp.arange(N_LOOP * N_GRP))
    return owners.reshape(QUERIES, HN).astype(jnp.int32)


def row_table(key):
    owners = owner_table(key)
    topics, unused = query_topics(key)
    layout = pool_layout(key)
    loop_index, group_index = query_blocks()
    owner_block = loop_index[:, None] * N_GRP + owners
    spread = jax.random.randint(jax.random.fold_in(key, 14), (QUERIES, HN), 0, POOL_DEV // topic_total())
    position = topics[:, None] + topic_total() * spread
    return layout[owner_block, position].astype(jnp.int32)


def noise_rows(key, salt, count):
    noise_key = jax.random.fold_in(key, salt)
    return jax.random.normal(noise_key, (count, D), jnp.float32)


def finish(mixed):
    return jnp.clip(mixed * 0.015625, -0.25, 0.25).astype(jnp.bfloat16)


def draw_passages(key, part):
    table = topic_table(key)
    mixed = table[passage_topics(key)] + noise_rows(key, 2, PASSAGES)
    return finish(mixed)


def draw_pool(key, part):
    table = topic_table(key)
    mixed = table[pool_topics(key)] + noise_rows(key, 3, POOL)
    return finish(mixed)


def draw_queries(key, part):
    table = topic_table(key)
    topics, source = query_topics(key)
    passage_noise = noise_rows(key, 2, PASSAGES)
    pool_noise = noise_rows(key, 3, POOL)
    owners = owner_table(key)
    pool_rows = row_table(key)
    loop_index, group_index = query_blocks()
    flat = (loop_index[:, None] * N_GRP + owners) * POOL_DEV + pool_rows
    mixed = table[topics]
    mixed = mixed + positive_share * passage_noise[source] + noise_share * noise_rows(key, 1, QUERIES)
    for column in range(HN):
        mixed = mixed + negative_share * pool_noise[flat[:, column]]
    return finish(mixed)


def draw_query_count(key, part):
    first, second = jax.random.split(jax.random.fold_in(key, 5))
    devices = N_LOOP * N_GRP
    counts = jax.random.randint(first, (devices,), max(1, Q_DEV // 4), Q_DEV + 1)
    full = jax.random.randint(second, (), 0, devices)
    counts = jnp.where(jnp.arange(devices) == full, Q_DEV, counts)
    return counts.reshape(N_LOOP, N_GRP).astype(jnp.int32)


def draw_positive(key, part):
    return positive_table(key)


def draw_neg_owner(key, part):
    return owner_table(key)


def draw_neg_row(key, part):
    return row_table(key)


def setup_inputs(seed: int = 0) -> dict:
    key_list = jax.random.split(jax.random.key(seed), 8)
    return {
        "queries": draw_queries(jax.random.fold_in(key_list[7], 71), 0),
        "passages": draw_passages(jax.random.fold_in(key_list[7], 71), 0),
        "pool": draw_pool(jax.random.fold_in(key_list[7], 71), 0),
        "query_count": draw_query_count(jax.random.fold_in(key_list[7], 71), 0),
        "positive": draw_positive(jax.random.fold_in(key_list[7], 71), 0),
        "neg_owner": draw_neg_owner(jax.random.fold_in(key_list[7], 71), 0),
        "neg_row": draw_neg_row(jax.random.fold_in(key_list[7], 71), 0),
    }


inv_temp = 50.0
eps = 1e-06

def unit_rows(rows):
    scale = lax.rsqrt(lax.optimization_barrier(jnp.sum(rows * rows, axis=-1, keepdims=True)) + eps)
    return (rows * scale, scale)

def unit_back(grad, unit, scale):
    return (grad - unit * lax.optimization_barrier(jnp.sum(unit * grad, axis=-1, keepdims=True))) * scale

def to_groups(x, inner):
    rest = x.shape[1:]
    shaped = x.reshape((N_LOOP, N_GRP, inner) + rest)
    order = (1, 0) + tuple(range(2, shaped.ndim))
    return shaped.transpose(order).reshape((N_GRP, N_LOOP * inner) + rest)

def from_groups(x, inner):
    rest = x.shape[2:]
    shaped = x.reshape((N_GRP, N_LOOP, inner) + rest)
    order = (1, 0) + tuple(range(2, shaped.ndim))
    return shaped.transpose(order).reshape((N_LOOP * N_GRP * inner,) + rest)

def reference(queries, passages, pool, query_count, positive, neg_owner, neg_row):
    q_unit, q_scale = unit_rows(queries.astype(jnp.float32))
    p_unit, p_scale = unit_rows(passages.astype(jnp.float32))
    n_unit, n_scale = unit_rows(pool.astype(jnp.float32))
    q_hat = q_unit.astype(jnp.bfloat16)
    p_hat = p_unit.astype(jnp.bfloat16)
    n_hat = n_unit.astype(jnp.bfloat16)
    live = jnp.arange(Q_DEV, dtype=jnp.int32)[None, None, :] < query_count[:, :, None]
    valid_groups = live.astype(jnp.float32).transpose(1, 0, 2).reshape(N_GRP, N_LOOP * Q_DEV)
    loop_of = jnp.arange(N_LOOP * Q_DEV, dtype=jnp.int32) // Q_DEV
    slots_in = N_LOOP * P_DEV
    columns = jnp.arange(slots_in, dtype=jnp.int32)

    def per_group(pool_sum, inputs):
        q_grp, p_grp, pos_grp, owner_grp, row_grp, valid_grp = inputs
        flat = ((loop_of[:, None] * N_GRP + owner_grp) * POOL_DEV + row_grp).astype(jnp.int32)
        negs = n_hat[flat]
        scores = jnp.dot(q_grp, p_grp.T, preferred_element_type=jnp.float32) * inv_temp
        hard = jnp.einsum('qd,qkd->qk', q_grp.astype(jnp.float32), negs.astype(jnp.float32)) * inv_temp
        weights_in = jnp.exp(scores - inv_temp)
        weights_hard = jnp.exp(hard - inv_temp)
        total = lax.optimization_barrier(jnp.sum(weights_in, axis=1)) + lax.optimization_barrier(jnp.sum(weights_hard, axis=1))
        chosen = jnp.take_along_axis(scores, pos_grp[:, None], axis=1)[:, 0]
        loss = valid_grp * (jnp.log(total) + inv_temp - chosen)
        target = (pos_grp[:, None] == columns[None, :]).astype(jnp.float32)
        valid_col = valid_grp[:, None]
        coef_in = (valid_col * (weights_in / total[:, None] - target)).astype(jnp.bfloat16)
        coef_hard = (valid_col * weights_hard / total[:, None]).astype(jnp.bfloat16)
        in_part = jnp.dot(coef_in, p_grp, preferred_element_type=jnp.float32)
        hard_part = jnp.einsum('qk,qkd->qd', coef_hard.astype(jnp.float32), negs.astype(jnp.float32))
        dq_hat = inv_temp * (in_part + hard_part)
        dp_hat = inv_temp * jnp.dot(coef_in.T, q_grp, preferred_element_type=jnp.float32)
        neg_grad = (inv_temp * coef_hard.astype(jnp.float32)[:, :, None] * q_grp.astype(jnp.float32)[:, None, :]).astype(jnp.bfloat16)
        pool_sum = pool_sum.at[flat.reshape(-1)].add(neg_grad.astype(jnp.float32).reshape(-1, D))
        return (pool_sum, (loss, dq_hat, dp_hat))
    inputs = (to_groups(q_hat, Q_DEV), to_groups(p_hat, P_DEV), to_groups(positive, Q_DEV), to_groups(neg_owner, Q_DEV), to_groups(neg_row, Q_DEV), valid_groups)
    start = jnp.zeros((POOL, D), jnp.float32)
    pool_sum, (loss, dq_hat, dp_hat) = lax.scan(per_group, start, inputs)
    loss = from_groups(loss, Q_DEV)
    grad_query = unit_back(from_groups(dq_hat, Q_DEV), q_unit, q_scale)
    grad_passage = unit_back(from_groups(dp_hat, P_DEV), p_unit, p_scale)
    grad_pool = unit_back(pool_sum, n_unit, n_scale)
    return (loss, grad_query, grad_passage, grad_pool)
```

```python
import functools

import jax
import jax.numpy as jnp
from jax import lax
from jax.experimental import pallas as pl
from jax.experimental.pallas import tpu as pltpu
from jax.sharding import PartitionSpec as P

inv_temp = 50.0
eps = 1e-06
f32 = jnp.float32
bf16 = jnp.bfloat16
vmem_bytes = 56 << 20
step_rows = 64


def hop_z(x, by):
    return lax.ppermute(x, "grp", [(g, (g + 4 * by) % 16) for g in range(16)])


def hop_xh(x):
    return lax.ppermute(x, "grp", [(g, g ^ 2) for g in range(16)])


def hop_core(x):
    return lax.ppermute(x, "grp", [(g, g ^ 1) for g in range(16)])


def hop_xl(x):
    return lax.ppermute(x, "loop", [(l, l ^ 4) for l in range(8)])


def hop_y(x, by):
    return lax.ppermute(x, "loop", [(l, (l & 4) + (l + by) % 4) for l in range(8)])


def after(values, *first):
    got = lax.optimization_barrier((tuple(values), first))
    return got[0]


def dot_nt(a, b):
    return lax.dot_general(a, b, (((1,), (1,)), ((), ())), preferred_element_type=f32)


def dot_nn(a, b):
    return lax.dot_general(a, b, (((1,), (0,)), ((), ())), preferred_element_type=f32)


def lane_squares(block):
    wide = block.astype(f32)
    wide = wide * wide
    part = wide[:, :128]
    for at in range(128, wide.shape[1], 128):
        part = part + wide[:, at : at + 128]
    return part


def inverse_norm(part):
    return lax.rsqrt(jnp.sum(part, axis=1, keepdims=True) + eps)


def stacked(refs):
    parts = [r[...] for r in refs]
    return parts[0] if len(parts) == 1 else jnp.concatenate(parts, axis=0)


def cols_spec(x, chunk=2048):
    return pl.BlockSpec((x.shape[0], chunk), lambda k: (0, k))


def whole_spec(x):
    return pl.BlockSpec(x.shape, lambda k: (0,) * x.ndim)


def smem_spec():
    return pl.BlockSpec(memory_space=pltpu.SMEM)


def cost(flops, *arrays, early=False):
    moved = sum(a.size * a.dtype.itemsize for a in arrays)
    if not early:
        flops, moved = 1, 1
    return pl.CostEstimate(flops=flops, bytes_accessed=moved, transcendentals=0)


def params():
    return pltpu.CompilerParams(vmem_limit_bytes=vmem_bytes)


def shape_of(shape, dtype):
    return jax.ShapeDtypeStruct(shape, dtype)


message_rows = 144
sizes = (128, 128, 64, 64, 128) * 2


def q_specs(q_refs, chunk):
    return [
        pl.BlockSpec((size, chunk), lambda k: (0, k)) for size, q in zip(sizes, q_refs)
    ]


def hard_kernel(bases, infos, before, *rest):
    q_refs = rest[:10]
    n1, n2, e1, e2, row_sum, s1, s2, codes, acc1, acc2, sq1, sq2 = rest[10:]
    k = pl.program_id(0)

    @pl.when(k == 0)
    def _():
        for ref in (acc1, acc2, sq1, sq2):
            ref[...] = jnp.zeros_like(ref)

    q_all = stacked(q_refs)
    for n, acc, sq in ((n1[...], acc1, sq1), (n2[...], acc2, sq2)):
        acc[...] += dot_nt(n, q_all)
        sq[...] += lane_squares(n)

    @pl.when(k == pl.num_programs(0) - 1)
    def _():
        for slot in range(8):
            info = infos[slot].astype(f32)
            code = info[0:8, 0:128] * 256.0 + info[8:16, 0:128]
            q_scale = info[0:1, 128:256] + info[1:2, 128:256] + info[2:3, 128:256]
            codes[slot] = jnp.concatenate([code[0:7], q_scale], axis=0)
        sums = [before[0:1, :]] + [jnp.zeros((1, 128), f32) for _ in range(7)]
        for h, (acc, sq, e, s) in enumerate(((acc1, sq1, e1, s1), (acc2, sq2, e2, s2))):
            scale = inverse_norm(sq[...])
            s[...] = jnp.broadcast_to(scale, s.shape)
            rows = lax.broadcasted_iota(jnp.int32, (acc.shape[0], 128), 0).astype(f32) + bases[h]
            for slot in range(8):
                lanes = slice(slot * 128, slot * 128 + 128)
                score = acc[:, lanes] * (scale * inv_temp) * codes[slot, 7:8, :]
                hits = jnp.zeros(rows.shape, f32)
                for which in range(7):
                    hits += jnp.where(rows == codes[slot, which : which + 1, :], 1.0, 0.0)
                weight = hits * jnp.exp(score)
                e[:, lanes] = weight
                sums[slot] += jnp.sum(weight, axis=0, keepdims=True)
        for slot in range(8):
            row_sum[slot : slot + 1, :] = sums[slot]


def hard_scores(bases, infos, before, q_refs, n1, n2, chunk=1024):
    rows, width = n1.shape
    outs = (
        shape_of((rows, 1024), f32),
        shape_of((rows, 1024), f32),
        shape_of((8, 128), f32),
        shape_of((rows, 128), f32),
        shape_of((rows, 128), f32),
        shape_of((8, 8, 128), f32),
    )
    return pl.pallas_call(
        hard_kernel,
        grid=(width // chunk,),
        in_specs=[smem_spec(), whole_spec(infos), whole_spec(before)]
        + q_specs(q_refs, chunk)
        + [cols_spec(x, chunk) for x in (n1, *n2)],
        out_specs=[whole_spec(o) for o in outs],
        out_shape=outs,
        scratch_shapes=[pltpu.VMEM((rows, 1024), f32)] * 2 + [pltpu.VMEM((rows, 128), f32)] * 2,
        compiler_params=params(),
        cost_estimate=cost(4 * rows * 1024 * width, n1, *n2, *q_refs, *outs[:2]),
        name="hard_scores",
    )(bases, infos, before, *q_refs, n1, *n2)


def passage_rows(refs):
    pc, p1, p2, p2x, p3 = [r[...] for r in refs]
    near = [pc[:64], p1[:64], p2, p3[:64]]
    far = [pc[64:], p1[64:], p2x, p3[64:]]
    return jnp.concatenate(near + far, axis=0)


def hot(places, pos, block):
    rows = lax.broadcasted_iota(jnp.int32, (64, pos.shape[1]), 0).astype(f32)
    return jnp.where(rows + places[block] == pos, 1.0, 0.0)


def batch_kernel(places, about, *rest):
    p_refs = rest[:5]
    q_refs = rest[5:-5]
    e, stats, scales, acc, sq = rest[-5:]
    k = pl.program_id(0)

    @pl.when(k == 0)
    def _():
        acc[...] = jnp.zeros_like(acc)
        sq[...] = jnp.zeros_like(sq)

    p_all = passage_rows(p_refs)
    acc[...] += dot_nt(p_all, stacked(q_refs))
    sq[...] += lane_squares(p_all)

    @pl.when(k == pl.num_programs(0) - 1)
    def _():
        scale = inverse_norm(sq[...])
        scales[...] = jnp.broadcast_to(scale, scales.shape)
        score = acc[...] * (scale * inv_temp) * about[0:1, :]
        weight = jnp.exp(score)
        e[...] = weight
        chosen = jnp.zeros((1, 128), f32)
        for block in range(8):
            part = score[block * 64 : block * 64 + 64]
            chosen += jnp.sum(part * hot(places, about[1:2, :], block), axis=0, keepdims=True)
        stats[0:1, :] = jnp.sum(weight, axis=0, keepdims=True)
        stats[1:2, :] = chosen
        stats[2:8, :] = jnp.zeros((6, 128), f32)


def batch_scores(places, about, p_refs, q_refs):
    width = q_refs[0].shape[1]
    outs = (shape_of((512, 128), f32), shape_of((8, 128), f32), shape_of((512, 128), f32))
    return pl.pallas_call(
        batch_kernel,
        grid=(width // 2048,),
        in_specs=[smem_spec(), whole_spec(about)] + [cols_spec(x) for x in (*p_refs, *q_refs)],
        out_specs=[whole_spec(o) for o in outs],
        out_shape=outs,
        scratch_shapes=[pltpu.VMEM((512, 128), f32), pltpu.VMEM((512, 128), f32)],
        compiler_params=params(),
        cost_estimate=cost(2 * 512 * 128 * width, *q_refs, *p_refs, *outs),
        name="batch_scores",
    )(places, about, *p_refs, *q_refs)


def back_kernel(first, e1, e2, s1, s2, n1, n2, *rest):
    turned = rest[-1]

    @pl.when(pl.program_id(0) == 0)
    def _():
        rows = e1.shape[0]
        turned[:, :rows] = jnp.transpose(e1[...] * s1[:, 0:1]).astype(bf16)
        turned[:, rows:] = jnp.transpose(e2[...] * s2[:, 0:1]).astype(bf16)

    part = dot_nn(turned[...], stacked([n1, n2]))
    if first:
        rest[0][...] = part.astype(bf16)
    else:
        got, home, u1, u2, u3 = rest[:5]
        part = part + got[...].astype(f32)
        home[...] = part[:128]
        for at, ref in enumerate((u1, u2, u3)):
            ref[...] = part[128 + at * 128 : 256 + at * 128].astype(bf16)


def hard_back(half, e1, e2, s1, s2, n1, n2, got=None):
    rows, width = n1.shape
    first = got is None
    if first:
        outs = (shape_of((512, width), bf16),)
        extra = ()
    else:
        outs = (shape_of((128, width), f32),) + (shape_of((128, width), bf16),) * 3
        extra = (got,)
    e_spec = pl.BlockSpec((rows, 512), lambda k: (0, half))
    return pl.pallas_call(
        functools.partial(back_kernel, first),
        grid=(width // 2048,),
        in_specs=[e_spec, e_spec, whole_spec(s1), whole_spec(s2)]
        + [cols_spec(x) for x in (n1, *n2, *extra)],
        out_specs=[cols_spec(o) for o in outs],
        out_shape=outs,
        scratch_shapes=[pltpu.VMEM((512, 2 * rows), bf16)],
        compiler_params=params(),
        cost_estimate=cost(2 * 512 * 2 * rows * width, n1, *n2, e1, *outs),
        name="hard_back",
    )(e1, e2, s1, s2, n1, *n2, *extra)


def pool_kernel(e, fac, *rest):
    q_refs = rest[:10]
    out, coef = rest[10:]

    @pl.when(pl.program_id(0) == 0)
    def _():
        for slot in range(8):
            lanes = slice(slot * 128, slot * 128 + 128)
            coef[:, lanes] = (e[:, lanes] * fac[slot : slot + 1, :]).astype(bf16)

    out[...] = dot_nn(coef[...], stacked(q_refs)).astype(out.dtype)


def pool_part(e, fac, q_refs, dtype):
    rows = e.shape[0]
    width = q_refs[0].shape[1]
    out = shape_of((rows, width), dtype)
    return pl.pallas_call(
        pool_kernel,
        grid=(width // 2048,),
        in_specs=[whole_spec(e), whole_spec(fac)] + q_specs(q_refs, 2048),
        out_specs=cols_spec(out),
        out_shape=out,
        scratch_shapes=[pltpu.VMEM((rows, 1024), bf16)],
        compiler_params=params(),
        cost_estimate=cost(2 * rows * 1024 * width, e, out, *q_refs),
        name="pool_part",
    )(e, fac, *q_refs)


def query_kernel(places, about, e, scales, *rest):
    p_refs = rest[:5]
    out, turned = rest[5:]

    @pl.when(pl.program_id(0) == 0)
    def _():
        for block in range(8):
            rows = slice(block * 64, block * 64 + 64)
            coef = e[rows, :] * about[0:1, :] - about[1:2, :] * hot(places, about[2:3, :], block)
            turned[rows, :] = coef * scales[rows, 0:1]

    turn = jnp.transpose(turned[...]).astype(bf16)
    out[...] = dot_nn(turn, passage_rows(p_refs))


def query_part(places, about, e, scales, p_refs):
    width = p_refs[0].shape[1]
    out = shape_of((128, width), f32)
    return pl.pallas_call(
        query_kernel,
        grid=(width // 2048,),
        in_specs=[smem_spec(), whole_spec(about), whole_spec(e), whole_spec(scales)]
        + [cols_spec(p) for p in p_refs],
        out_specs=cols_spec(out),
        out_shape=out,
        scratch_shapes=[pltpu.VMEM((512, 128), f32)],
        compiler_params=params(),
        cost_estimate=cost(2 * 512 * 128 * width, out, *p_refs),
        name="query_part",
    )(places, about, e, scales, *p_refs)


def passage_kernel(places, about_a, about_b, e_a, e_b, q_a, q_b, q_c, home, d1, d2, d3, coef):
    @pl.when(pl.program_id(0) == 0)
    def _():
        for at, (about, e) in enumerate(((about_a, e_a), (about_b, e_b))):
            lanes = slice(at * 128, at * 128 + 128)
            for block in range(4):
                rows = slice(block * 64, block * 64 + 64)
                part = e[rows, :] * about[0:1, :] - about[1:2, :] * hot(places, about[2:3, :], block)
                coef[rows, lanes] = (part * about[3:4, :]).astype(bf16)

    part = dot_nn(coef[...], stacked([q_a, q_b, q_c]))
    home[...] = part[:64]
    for at, ref in enumerate((d1, d2, d3)):
        ref[...] = part[64 + at * 64 : 128 + at * 64].astype(bf16)


def passage_part(places, about_a, about_b, e_a, e_b, q_a, q_b):
    width = q_a.shape[1]
    outs = (shape_of((64, width), f32),) + (shape_of((64, width), bf16),) * 3
    near = pl.BlockSpec((256, 128), lambda k: (0, 0))
    return pl.pallas_call(
        passage_kernel,
        grid=(width // 2048,),
        in_specs=[smem_spec(), whole_spec(about_a), whole_spec(about_b), near, near]
        + [cols_spec(x) for x in (q_a, *q_b)],
        out_specs=[cols_spec(o) for o in outs],
        out_shape=outs,
        scratch_shapes=[pltpu.VMEM((256, 256), bf16)],
        compiler_params=params(),
        cost_estimate=cost(2 * 256 * 256 * width, q_a, *q_b, *outs),
        name="passage_part",
    )(places, about_a, about_b, e_a, e_b, q_a, *q_b)


def last_kernel(n_parts, has_fac, *refs):
    parts = refs[:n_parts]
    rest = list(refs[n_parts:])
    total = None
    for ref in parts:
        pieces = [ref[...]] if len(ref.shape) == 2 else [ref[i] for i in range(ref.shape[0])]
        for piece in pieces:
            piece = piece.astype(f32)
            total = piece if total is None else total + piece
    if has_fac:
        fac, plain = rest[0], rest[1]
        total = total * fac[:, 0:1] + plain[...]
        rest = rest[2:]
    raw, out = rest[0], rest[-1]
    rows = raw[...].astype(f32)
    scale = lax.rsqrt(jnp.sum(rows * rows, axis=1, keepdims=True) + eps)
    along = jnp.sum(rows * total, axis=1, keepdims=True) * (scale * scale)
    out[...] = (total - rows * along) * (scale * inv_temp)


def last_step(parts, raw, fac=None, plain=None, step=step_rows):
    width = raw.shape[1]
    rows = raw.shape[0]

    def spec(x):
        if len(x.shape) == 3:
            return pl.BlockSpec((x.shape[0], step, x.shape[2]), lambda i: (0, i, 0))
        return pl.BlockSpec((step, x.shape[1]), lambda i: (i, 0))

    extra = () if fac is None else (fac, plain)
    ins = (*parts, *extra, raw)
    out = shape_of(raw.shape, f32)
    return pl.pallas_call(
        functools.partial(last_kernel, len(parts), fac is not None),
        grid=(rows // step,),
        in_specs=[spec(x) for x in ins],
        out_specs=spec(out),
        out_shape=out,
        compiler_params=params(),
        cost_estimate=cost(8 * rows * width, out, *ins),
        name="last_step",
    )(*ins)


def local(queries, passages, pool, query_count, positive, neg_owner, neg_row):
    n_query = queries.shape[0]
    n_pool = pool.shape[0]
    grp = lax.axis_index("grp")
    loop = lax.axis_index("loop")
    zi, xh, ci = grp // 4, (grp // 2) % 2, grp % 2
    xl, yi = loop // 4, loop % 4

    valid = (lax.iota(jnp.int32, n_query) < query_count.reshape(())).astype(f32)
    wide = queries.astype(f32)
    q_scale = lax.rsqrt(jnp.sum(wide * wide, axis=1) + eps)
    high = lax.reduce_precision(q_scale, 8, 7)
    mid = lax.reduce_precision(q_scale - high, 8, 7)
    low = q_scale - high - mid
    zero_row = jnp.zeros((1, n_query), f32)
    owners = jnp.where(valid[None, :] > 0, neg_owner.T.astype(f32), -1.0)
    left = jnp.concatenate([owners, zero_row, neg_row.T.astype(f32), zero_row], axis=0)
    right = jnp.concatenate([high[None], mid[None], low[None], jnp.tile(zero_row, (13, 1))], axis=0)
    info = jnp.concatenate([left, right], axis=1).astype(bf16)
    info = jnp.pad(info, ((0, 0), (0, queries.shape[1] - 2 * n_query)))
    message = jnp.concatenate([queries, info], axis=0)

    px = hop_xl(passages)
    q1 = hop_z(message, -1)
    q3 = hop_z(message, 1)
    side0 = hop_core(message)
    pool_late, passages_late = after((pool, passages), px)
    pool_x = (hop_xh(pool_late),)
    pc = jnp.concatenate([passages_late, px], axis=0)
    p1 = hop_y(pc, -1)
    p3 = hop_y(pc, 1)
    q1_next, q3_next = after((q1, q3), pc)
    q2a = hop_z(q1_next[:64], -1)
    q2b = hop_z(q3_next[64:], 1)
    p2 = hop_y(p1[:64], -1)
    p2x = hop_y(p3[64:], 1)
    q1_late, q3_late = after((q1, q3), q2a, q2b)
    side1, side3 = hop_core(q1_late), hop_core(q3_late)
    side2a, side2b = hop_core(q2a), hop_core(q2b)
    q_refs = (message, q1, q2a, q2b, q3, side0, side1, side2a, side2b, side3)
    p_refs = (pc, p1, p2, p2x, p3)
    tails = (message[128:], q1[128:], q2b[64:], q3[128:], side0[128:], side1[128:], side2b[64:], side3[128:])
    infos = jnp.stack([x[:, :256] for x in tails])

    bases = jnp.stack([grp * n_pool, (grp ^ 2) * n_pool]).astype(f32)
    steps = jnp.arange(4, dtype=jnp.int32)
    y_places = (yi + steps) % 4
    places = (
        jnp.concatenate([xl * 4 + y_places, (1 - xl) * 4 + y_places]) * passages.shape[0]
    ).astype(f32)
    pos = positive.astype(f32)
    about_first = jnp.concatenate([q_scale[None], pos[None], jnp.tile(zero_row, (6, 1))], axis=0)

    e_batch, stats, p_scales = batch_scores(places, about_first, p_refs, (queries,))
    e1, e2, part, s1, s2, codes = hard_scores(bases, infos, stats, q_refs, pool, pool_x)
    q_late, about_late = after((queries, about_first), pool_x[0])
    q_xa = hop_xl(q_late[:64])
    about_first_x = hop_xl(about_late)

    (e1_side, e2_side) = after((e1, e2), part, q_xa, about_first_x)
    (q_later,) = after((queries,), q_xa)
    q_xb = hop_xl(q_later[64:])
    got = [hop_z(part, -by) for by in (1, 2, 3)]
    (u_side,) = hard_back(1, e1_side, e2_side, s1, s2, pool, pool_x)
    u_got = hop_core(u_side)
    got, _ = lax.optimization_barrier((got, u_side))
    total = part.reshape(2, 4, n_query)
    for by in (1, 2, 3):
        total = total + jnp.roll(got[by - 1].reshape(2, 4, n_query), by, axis=1)
    core_total = hop_core(total)
    total = total + core_total[::-1]
    live = (codes[:, 0, :] >= 0).astype(f32)
    fac = live * codes[:, 7, :] / total.reshape(8, n_query)
    own_total = total[0, 0]
    loss = valid * (jnp.log(own_total) - stats[1])
    own_fac = valid / own_total
    about = jnp.concatenate(
        [own_fac[None], valid[None], pos[None], q_scale[None], jnp.tile(zero_row, (4, 1))], axis=0
    )
    about_x = hop_xl(about)

    dn_far = pool_part(e2, fac, q_refs, bf16)
    dn_far, _ = lax.optimization_barrier((dn_far, (about_x, q_xb)))
    dn_x = hop_xh(dn_far)
    (u_got,) = after((u_got,), dn_far)
    u_home, u1, u2, u3 = hard_back(0, e1, e2, s1, s2, pool, pool_x, u_got)
    u_parts = (u_home, hop_z(u1, 1), hop_z(u2, 2), hop_z(u3, -1))
    q_x = after((q_xa, q_xb), u_home)
    e_batch_x, _, _ = batch_scores(places, about_first_x, p_refs, q_x)
    d_home, d1, d2, d3 = passage_part(places, about, about_x, e_batch, e_batch_x, queries, q_x)
    d_parts = (d_home, hop_y(d1, 1), hop_y(d2, 2), hop_y(d3, -1))

    (e1_late, e_late) = after((e1, e_batch), d_home)
    dn_home = pool_part(e1_late, fac, q_refs, f32)
    dq_batch = query_part(places, about, e_late, p_scales, p_refs)
    grad_passage = last_step(d_parts, passages)
    fac_rows = jnp.broadcast_to(own_fac[:, None], (n_query, 128))
    (dn_x,) = after((dn_x,), grad_passage)
    grad_pool = last_step((dn_home, dn_x), pool)
    (dq_batch,) = after((dq_batch,), grad_pool)
    grad_query = last_step(u_parts, queries, fac_rows, dq_batch)
    return (loss, grad_query, grad_passage, grad_pool)


def solution(mesh):
    both = ("loop", "grp")
    return jax.shard_map(
        local,
        mesh=mesh,
        in_specs=(
            P(both, None),
            P(both, None),
            P(both, None),
            P("loop", "grp"),
            P(both),
            P(both, None),
            P(both, None),
        ),
        out_specs=(P(both), P(both, None), P(both, None), P(both, None)),
        check_vma=False,
    )
```

```python
import functools

import jax
import jax.numpy as jnp
from jax import lax
from jax.experimental import pallas as pl
from jax.experimental.pallas import tpu as pltpu
from jax.sharding import PartitionSpec as P

inv_temp = 50.0
eps = 1e-06
f32 = jnp.float32
bf16 = jnp.bfloat16
vmem_bytes = 56 << 20
step_rows = 64


def hop_z(x, by):
    return lax.ppermute(x, "grp", [(g, (g + 4 * by) % 16) for g in range(16)])


def hop_xh(x):
    return lax.ppermute(x, "grp", [(g, g ^ 2) for g in range(16)])


def hop_core(x):
    return lax.ppermute(x, "grp", [(g, g ^ 1) for g in range(16)])


def hop_xl(x):
    return lax.ppermute(x, "loop", [(l, l ^ 4) for l in range(8)])


def hop_y(x, by):
    return lax.ppermute(x, "loop", [(l, (l & 4) + (l + by) % 4) for l in range(8)])


def after(values, *first):
    got = lax.optimization_barrier((tuple(values), first))
    return got[0]


def dot_nt(a, b):
    return lax.dot_general(a, b, (((1,), (1,)), ((), ())), preferred_element_type=f32)


def dot_nn(a, b):
    return lax.dot_general(a, b, (((1,), (0,)), ((), ())), preferred_element_type=f32)


def lane_squares(block):
    wide = block.astype(f32)
    wide = wide * wide
    part = wide[:, :128]
    for at in range(128, wide.shape[1], 128):
        part = part + wide[:, at : at + 128]
    return part


def inverse_norm(part):
    return lax.rsqrt(jnp.sum(part, axis=1, keepdims=True) + eps)


def stacked(refs):
    parts = [r[...] for r in refs]
    return parts[0] if len(parts) == 1 else jnp.concatenate(parts, axis=0)


def cols_spec(x, chunk=2048):
    return pl.BlockSpec((x.shape[0], chunk), lambda k: (0, k))


def whole_spec(x):
    return pl.BlockSpec(x.shape, lambda k: (0,) * x.ndim)


def smem_spec():
    return pl.BlockSpec(memory_space=pltpu.SMEM)


def cost(flops, *arrays, early=False):
    moved = sum(a.size * a.dtype.itemsize for a in arrays)
    if not early:
        flops, moved = 1, 1
    return pl.CostEstimate(flops=flops, bytes_accessed=moved, transcendentals=0)


def params():
    return pltpu.CompilerParams(vmem_limit_bytes=vmem_bytes)


def shape_of(shape, dtype):
    return jax.ShapeDtypeStruct(shape, dtype)


message_rows = 144
sizes = (128, 128, 64, 64, 128) * 2


def q_specs(q_refs, chunk):
    return [
        pl.BlockSpec((size, chunk), lambda k: (0, k)) for size, q in zip(sizes, q_refs)
    ]


def hard_kernel(bases, *rest):
    infos, rest = rest[:8], rest[8:]
    q_refs = rest[:10]
    n1, n2, e1, e2, row_sum, s1, s2, codes, acc1, acc2, sq1, sq2 = rest[10:]
    k = pl.program_id(0)

    @pl.when(k == 0)
    def _():
        for ref in (acc1, acc2, sq1, sq2):
            ref[...] = jnp.zeros_like(ref)

    q_all = stacked(q_refs)
    for n, acc, sq in ((n1[...], acc1, sq1), (n2[...], acc2, sq2)):
        acc[...] += dot_nt(n, q_all)
        sq[...] += lane_squares(n)

    @pl.when(k == pl.num_programs(0) - 1)
    def _():
        for slot in range(8):
            info = infos[slot][...].astype(f32)
            code = info[0:8, 0:128] * 256.0 + info[8:16, 0:128]
            q_scale = info[0:1, 128:256] + info[1:2, 128:256] + info[2:3, 128:256]
            codes[slot] = jnp.concatenate([code[0:7], q_scale], axis=0)
        sums = [jnp.zeros((1, 128), f32) for _ in range(8)]
        for h, (acc, sq, e, s) in enumerate(((acc1, sq1, e1, s1), (acc2, sq2, e2, s2))):
            scale = inverse_norm(sq[...])
            s[...] = jnp.broadcast_to(scale, s.shape)
            rows = lax.broadcasted_iota(jnp.int32, (acc.shape[0], 128), 0).astype(f32) + bases[h]
            for slot in range(8):
                lanes = slice(slot * 128, slot * 128 + 128)
                score = acc[:, lanes] * (scale * inv_temp) * codes[slot, 7:8, :]
                hits = jnp.zeros(rows.shape, f32)
                for which in range(7):
                    hits += jnp.where(rows == codes[slot, which : which + 1, :], 1.0, 0.0)
                weight = hits * jnp.exp(score)
                e[:, lanes] = weight
                sums[slot] += jnp.sum(weight, axis=0, keepdims=True)
        for slot in range(8):
            row_sum[slot : slot + 1, :] = sums[slot]


def hard_scores(bases, q_refs, n1, n2, chunk=1024):
    rows, width = n1.shape
    tails = [q for q in q_refs if q.shape[0] % 128 == 16 or q.shape[0] % 64 == 16]
    outs = (
        shape_of((rows, 1024), f32),
        shape_of((rows, 1024), f32),
        shape_of((8, 128), f32),
        shape_of((rows, 128), f32),
        shape_of((rows, 128), f32),
        shape_of((8, 8, 128), f32),
    )
    return pl.pallas_call(
        hard_kernel,
        grid=(width // chunk,),
        in_specs=[smem_spec()]
        + [pl.BlockSpec((16, 256), lambda k, at=x.shape[0] // 16 - 1: (at, 0)) for x in tails]
        + q_specs(q_refs, chunk)
        + [cols_spec(x, chunk) for x in (n1, *n2)],
        out_specs=[whole_spec(o) for o in outs],
        out_shape=outs,
        scratch_shapes=[pltpu.VMEM((rows, 1024), f32)] * 2 + [pltpu.VMEM((rows, 128), f32)] * 2,
        compiler_params=params(),
        cost_estimate=cost(4 * rows * 1024 * width, n1, *n2, *q_refs, *outs[:2]),
        name="hard_scores",
    )(bases, *tails, *q_refs, n1, *n2)


def hot(start, count, pos):
    rows = lax.broadcasted_iota(jnp.int32, (count, pos.shape[1]), 0) + start
    return jnp.where(rows.astype(f32) == pos, 1.0, 0.0)


def hot_all(places, pos):
    return jnp.concatenate([hot(places[block], 64, pos) for block in range(8)], axis=0)


def batch_kernel(places, about, sums, p_all, *rest):
    q_refs = rest[:-6]
    e, total, stats, scales, acc, sq = rest[-6:]
    k = pl.program_id(0)

    @pl.when(k == 0)
    def _():
        acc[...] = jnp.zeros_like(acc)
        sq[...] = jnp.zeros_like(sq)

    acc[...] += dot_nt(p_all[...], stacked(q_refs))
    sq[...] += lane_squares(p_all[...])

    @pl.when(k == pl.num_programs(0) - 1)
    def _():
        scale = inverse_norm(sq[...])
        scales[...] = jnp.broadcast_to(scale, scales.shape)
        score = acc[...] * (scale * inv_temp) * about[0:1, :]
        weight = jnp.exp(score)
        e[...] = weight
        total[0:1, :] = sums[0:1, :] + jnp.sum(weight, axis=0, keepdims=True)
        total[1:8, :] = sums[1:8, :]
        chosen = score * hot_all(places, about[1:2, :])
        stats[...] = jnp.broadcast_to(jnp.sum(chosen, axis=0, keepdims=True), stats.shape)


def batch_scores(places, about, sums, p_all, q_refs):
    rows, width = p_all.shape
    outs = (
        shape_of((rows, 128), f32),
        shape_of((8, 128), f32),
        shape_of((8, 128), f32),
        shape_of((rows, 128), f32),
    )
    return pl.pallas_call(
        batch_kernel,
        grid=(width // 2048,),
        in_specs=[smem_spec(), whole_spec(about), whole_spec(sums)]
        + [cols_spec(x) for x in (p_all, *q_refs)],
        out_specs=[whole_spec(o) for o in outs],
        out_shape=outs,
        scratch_shapes=[pltpu.VMEM((rows, 128), f32), pltpu.VMEM((rows, 128), f32)],
        compiler_params=params(),
        cost_estimate=cost(2 * rows * 128 * width, p_all, *q_refs, *outs),
        name="batch_scores",
    )(places, about, sums, p_all, *q_refs)


def back_kernel(first, e1, e2, s1, s2, n1, n2, *rest):
    turned = rest[-1]

    @pl.when(pl.program_id(0) == 0)
    def _():
        rows = e1.shape[0]
        turned[:, :rows] = jnp.transpose(e1[...] * s1[:, 0:1]).astype(bf16)
        turned[:, rows:] = jnp.transpose(e2[...] * s2[:, 0:1]).astype(bf16)

    part = dot_nn(turned[...], stacked([n1, n2]))
    if first:
        rest[0][...] = part.astype(bf16)
    else:
        got, home, u1, u2, u3 = rest[:5]
        part = part + got[...].astype(f32)
        home[...] = part[:128]
        for at, ref in enumerate((u1, u2, u3)):
            ref[...] = part[128 + at * 128 : 256 + at * 128].astype(bf16)


def hard_back(half, e1, e2, s1, s2, n1, n2, got=None):
    rows, width = n1.shape
    first = got is None
    if first:
        outs = (shape_of((512, width), bf16),)
        extra = ()
    else:
        outs = (shape_of((128, width), f32),) + (shape_of((128, width), bf16),) * 3
        extra = (got,)
    e_spec = pl.BlockSpec((rows, 512), lambda k: (0, half))
    return pl.pallas_call(
        functools.partial(back_kernel, first),
        grid=(width // 2048,),
        in_specs=[e_spec, e_spec, whole_spec(s1), whole_spec(s2)]
        + [cols_spec(x) for x in (n1, *n2, *extra)],
        out_specs=[cols_spec(o) for o in outs],
        out_shape=outs,
        scratch_shapes=[pltpu.VMEM((512, 2 * rows), bf16)],
        compiler_params=params(),
        cost_estimate=cost(2 * 512 * 2 * rows * width, n1, *n2, e1, *outs),
        name="hard_back",
    )(e1, e2, s1, s2, n1, *n2, *extra)


def pool_kernel(e, fac, *rest):
    q_refs = rest[:10]
    out, coef = rest[10:]

    @pl.when(pl.program_id(0) == 0)
    def _():
        for slot in range(8):
            lanes = slice(slot * 128, slot * 128 + 128)
            coef[:, lanes] = (e[:, lanes] * fac[slot : slot + 1, :]).astype(bf16)

    out[...] = dot_nn(coef[...], stacked(q_refs)).astype(out.dtype)


def pool_part(e, fac, q_refs, dtype):
    rows = e.shape[0]
    width = q_refs[0].shape[1]
    out = shape_of((rows, width), dtype)
    return pl.pallas_call(
        pool_kernel,
        grid=(width // 2048,),
        in_specs=[whole_spec(e), whole_spec(fac)] + q_specs(q_refs, 2048),
        out_specs=cols_spec(out),
        out_shape=out,
        scratch_shapes=[pltpu.VMEM((rows, 1024), bf16)],
        compiler_params=params(),
        cost_estimate=cost(2 * rows * 1024 * width, e, out, *q_refs),
        name="pool_part",
    )(e, fac, *q_refs)


def query_kernel(places, about, e, scales, p_all, out, turned):
    @pl.when(pl.program_id(0) == 0)
    def _():
        target = hot_all(places, about[2:3, :])
        coef = (e[...] * about[0:1, :] - about[1:2, :] * target) * scales[:, 0:1]
        turned[...] = jnp.transpose(coef).astype(bf16)

    out[...] = dot_nn(turned[...], p_all[...])


def query_part(places, about, e, scales, p_all):
    rows, width = p_all.shape
    out = shape_of((128, width), f32)
    return pl.pallas_call(
        query_kernel,
        grid=(width // 2048,),
        in_specs=[smem_spec()] + [whole_spec(x) for x in (about, e, scales)] + [cols_spec(p_all)],
        out_specs=cols_spec(out),
        out_shape=out,
        scratch_shapes=[pltpu.VMEM((128, rows), bf16)],
        compiler_params=params(),
        cost_estimate=cost(2 * rows * 128 * width, out, p_all),
        name="query_part",
    )(places, about, e, scales, p_all)


def passage_kernel(turns, places, about_a, about_b, e_a, e_b, *rest):
    home, d1, d2, d3, coef = rest[-5:]
    q_refs = rest[:-5]

    @pl.when(pl.program_id(0) == 0)
    def _():
        for at, (about, e) in enumerate(((about_a, e_a), (about_b, e_b))):
            lanes = slice(at * 128, at * 128 + 128)
            for block in range(4):
                start = pl.multiple_of(turns[block] * 128, 128)
                target = hot(places[2 * turns[block]], 64, about[2:3, :])
                part = e[pl.ds(start, 64), :] * about[0:1, :] - about[1:2, :] * target
                coef[block * 64 : block * 64 + 64, lanes] = (part * about[3:4, :]).astype(bf16)

    part = dot_nn(coef[...], stacked(q_refs))
    home[...] = part[:64]
    for at, ref in enumerate((d1, d2, d3)):
        ref[...] = part[64 + at * 64 : 128 + at * 64].astype(bf16)


def passage_part(turns, places, about_a, about_b, e_a, e_b, q_refs):
    width = q_refs[0].shape[1]
    outs = (shape_of((64, width), f32),) + (shape_of((64, width), bf16),) * 3
    return pl.pallas_call(
        passage_kernel,
        grid=(width // 2048,),
        in_specs=[smem_spec(), smem_spec()]
        + [whole_spec(x) for x in (about_a, about_b, e_a, e_b)]
        + [cols_spec(x) for x in q_refs],
        out_specs=[cols_spec(o) for o in outs],
        out_shape=outs,
        scratch_shapes=[pltpu.VMEM((256, 256), bf16)],
        compiler_params=params(),
        cost_estimate=cost(2 * 256 * 256 * width, *q_refs, *outs),
        name="passage_part",
    )(turns, places, about_a, about_b, e_a, e_b, *q_refs)


def last_kernel(n_parts, has_fac, *refs):
    parts = refs[:n_parts]
    rest = list(refs[n_parts:])
    total = None
    for ref in parts:
        pieces = [ref[...]] if len(ref.shape) == 2 else [ref[i] for i in range(ref.shape[0])]
        for piece in pieces:
            piece = piece.astype(f32)
            total = piece if total is None else total + piece
    if has_fac:
        fac, plain = rest[0], rest[1]
        total = total * fac[:, 0:1] + plain[...]
        rest = rest[2:]
    raw, out = rest[0], rest[-1]
    rows = raw[...].astype(f32)
    scale = lax.rsqrt(jnp.sum(rows * rows, axis=1, keepdims=True) + eps)
    along = jnp.sum(rows * total, axis=1, keepdims=True) * (scale * scale)
    out[...] = (total - rows * along) * (scale * inv_temp)


def last_step(parts, raw, fac=None, plain=None, step=step_rows):
    width = raw.shape[1]
    rows = raw.shape[0]

    def spec(x):
        if len(x.shape) == 3:
            return pl.BlockSpec((x.shape[0], step, x.shape[2]), lambda i: (0, i, 0))
        return pl.BlockSpec((step, x.shape[1]), lambda i: (i, 0))

    extra = () if fac is None else (fac, plain)
    ins = (*parts, *extra, raw)
    out = shape_of(raw.shape, f32)
    return pl.pallas_call(
        functools.partial(last_kernel, len(parts), fac is not None),
        grid=(rows // step,),
        in_specs=[spec(x) for x in ins],
        out_specs=spec(out),
        out_shape=out,
        compiler_params=params(),
        cost_estimate=cost(8 * rows * width, out, *ins),
        name="last_step",
    )(*ins)


def local(queries, passages, pool, query_count, positive, neg_owner, neg_row):
    n_query = queries.shape[0]
    n_pool = pool.shape[0]
    grp = lax.axis_index("grp")
    loop = lax.axis_index("loop")
    zi, xh, ci = grp // 4, (grp // 2) % 2, grp % 2
    xl, yi = loop // 4, loop % 4

    valid = (lax.iota(jnp.int32, n_query) < query_count.reshape(())).astype(f32)
    wide = queries.astype(f32)
    q_scale = lax.rsqrt(jnp.sum(wide * wide, axis=1) + eps)
    high = lax.reduce_precision(q_scale, 8, 7)
    mid = lax.reduce_precision(q_scale - high, 8, 7)
    low = q_scale - high - mid
    zero_row = jnp.zeros((1, n_query), f32)
    owners = jnp.where(valid[None, :] > 0, neg_owner.T.astype(f32), -1.0)
    left = jnp.concatenate([owners, zero_row, neg_row.T.astype(f32), zero_row], axis=0)
    right = jnp.concatenate([high[None], mid[None], low[None], jnp.tile(zero_row, (13, 1))], axis=0)
    info = jnp.concatenate([left, right], axis=1).astype(bf16)
    info = jnp.pad(info, ((0, 0), (0, queries.shape[1] - 2 * n_query)))
    message = jnp.concatenate([queries, info], axis=0)

    px = hop_xl(passages)
    q1 = hop_z(message, -1)
    q3 = hop_z(message, 1)
    pool_late, px_late, passages_late = after((pool, px, passages), px, message)
    pool_x = (hop_xh(pool_late),)
    pc = jnp.concatenate([passages_late, px_late], axis=0)
    y_groups = [[l * 4 + y for y in range(4)] for l in range(2)]
    p_all = lax.all_gather(pc, "loop", axis=0, tiled=True, axis_index_groups=y_groups)
    side0 = hop_core(message)
    q2a = hop_z(q1[:64], -1)
    q2b = hop_z(q3[64:], 1)
    q1_late, q3_late = after((q1, q3), q2a, q2b)
    side1, side3 = hop_core(q1_late), hop_core(q3_late)
    side2a, side2b = hop_core(q2a), hop_core(q2b)
    q_refs = (message, q1, q2a, q2b, q3, side0, side1, side2a, side2b, side3)
    bases = jnp.stack([grp * n_pool, (grp ^ 2) * n_pool]).astype(f32)
    steps = jnp.arange(4, dtype=jnp.int32)
    turns = (yi + steps) % 4
    places = jnp.stack([xl * 4 + steps, (1 - xl) * 4 + steps], axis=1).reshape(8) * passages.shape[0]
    pos = positive.astype(f32)
    about_first = jnp.concatenate([q_scale[None], pos[None], jnp.tile(zero_row, (6, 1))], axis=0)

    e1, e2, hard_sums, s1, s2, codes = hard_scores(bases, q_refs, pool, pool_x)
    q_late, about_late = after((queries, about_first), pool_x[0])
    q_xa = hop_xl(q_late[:64])
    about_first_x = hop_xl(about_late)
    (e1_side,) = after((e1,), q_xa, about_first_x)
    (q_later,) = after((queries,), q_xa)
    q_xb = hop_xl(q_later[64:])
    (u_side,) = hard_back(1, e1_side, e2, s1, s2, pool, pool_x)
    u_got = hop_core(u_side)
    (hard_sums,) = after((hard_sums,), u_side)
    e_batch, part, chosen, p_scales = batch_scores(places, about_first, hard_sums, p_all, (queries,))

    got = [hop_z(part, -by) for by in (1, 2, 3)]
    got, _ = lax.optimization_barrier((got, u_side))
    total = part.reshape(2, 4, n_query)
    for by in (1, 2, 3):
        total = total + jnp.roll(got[by - 1].reshape(2, 4, n_query), by, axis=1)
    core_total = hop_core(total)
    total = total + core_total[::-1]
    live = (codes[:, 0, :] >= 0).astype(f32)
    fac = live * codes[:, 7, :] / total.reshape(8, n_query)
    own_total = total[0, 0]
    loss = valid * (jnp.log(own_total) - chosen[0])
    own_fac = valid / own_total
    about = jnp.concatenate(
        [own_fac[None], valid[None], pos[None], q_scale[None], jnp.tile(zero_row, (4, 1))], axis=0
    )
    about_x = hop_xl(about)

    dn_far = pool_part(e2, fac, q_refs, bf16)
    dn_far, _ = lax.optimization_barrier((dn_far, (about_x, q_xb)))
    dn_x = hop_xh(dn_far)
    (u_got,) = after((u_got,), dn_far)
    u_home, u1, u2, u3 = hard_back(0, e1, e2, s1, s2, pool, pool_x, u_got)
    u_parts = (u_home, hop_z(u1, 1), hop_z(u2, 2), hop_z(u3, -1))
    q_xa, q_xb = after((q_xa, q_xb), u_home)
    e_batch_x, _, _, _ = batch_scores(places, about_first_x, hard_sums, p_all, (q_xa, q_xb))
    d_home, d1, d2, d3 = passage_part(
        turns, places, about, about_x, e_batch, e_batch_x, (queries, q_xa, q_xb)
    )
    (e1_late,) = after((e1,), d_home)
    dn_home = pool_part(e1_late, fac, q_refs, f32)
    (e_late,) = after((e_batch,), dn_home)
    dq_batch = query_part(places, about, e_late, p_scales, p_all)
    fac_rows = jnp.broadcast_to(own_fac[:, None], (n_query, 128))
    d_one = hop_y(d1, 1)
    grad_pool = last_step((dn_home, dn_x), pool)
    (d2, d3, dq_batch) = after((d2, d3, dq_batch), grad_pool, d_one)
    d_two = hop_y(d2, 2)
    d_three = hop_y(d3, -1)
    grad_query = last_step(u_parts, queries, fac_rows, dq_batch)
    (d_one, d_two, d_three), _ = lax.optimization_barrier(((d_one, d_two, d_three), grad_query))
    grad_passage = last_step((d_home, d_one, d_two, d_three), passages)
    return (loss, grad_query, grad_passage, grad_pool)


def solution(mesh):
    both = ("loop", "grp")
    return jax.shard_map(
        local,
        mesh=mesh,
        in_specs=(
            P(both, None),
            P(both, None),
            P(both, None),
            P("loop", "grp"),
            P(both),
            P(both, None),
            P(both, None),
        ),
        out_specs=(P(both), P(both, None), P(both, None), P(both, None)),
        check_vma=False,
    )
```

```python
import functools

import jax
import jax.numpy as jnp
from jax import lax
from jax.experimental import pallas as pl
from jax.experimental.pallas import tpu as pltpu
from jax.sharding import PartitionSpec as P

inv_temp = 50.0
eps = 1e-06
f32 = jnp.float32
bf16 = jnp.bfloat16
vmem_bytes = 56 << 20
step_rows = 64


def hop_z(x, by):
    return lax.ppermute(x, "grp", [(g, (g + 4 * by) % 16) for g in range(16)])


def hop_xh(x):
    return lax.ppermute(x, "grp", [(g, g ^ 2) for g in range(16)])


def hop_core(x):
    return lax.ppermute(x, "grp", [(g, g ^ 1) for g in range(16)])


def hop_xl(x):
    return lax.ppermute(x, "loop", [(l, l ^ 4) for l in range(8)])


def hop_y(x, by):
    return lax.ppermute(x, "loop", [(l, (l & 4) + (l + by) % 4) for l in range(8)])


def after(values, *first):
    got = lax.optimization_barrier((tuple(values), first))
    return got[0]


def dot_nt(a, b):
    return lax.dot_general(a, b, (((1,), (1,)), ((), ())), preferred_element_type=f32)


def dot_nn(a, b):
    return lax.dot_general(a, b, (((1,), (0,)), ((), ())), preferred_element_type=f32)


def lane_squares(block):
    wide = block.astype(f32)
    wide = wide * wide
    part = wide[:, :128]
    for at in range(128, wide.shape[1], 128):
        part = part + wide[:, at : at + 128]
    return part


def inverse_norm(part):
    return lax.rsqrt(jnp.sum(part, axis=1, keepdims=True) + eps)


def stacked(refs):
    parts = [r[...] for r in refs]
    return parts[0] if len(parts) == 1 else jnp.concatenate(parts, axis=0)


def cols_spec(x, chunk=2048):
    return pl.BlockSpec((x.shape[0], chunk), lambda k: (0, k))


def whole_spec(x):
    return pl.BlockSpec(x.shape, lambda k: (0,) * x.ndim)


def smem_spec():
    return pl.BlockSpec(memory_space=pltpu.SMEM)


def cost(flops, *arrays, early=False):
    moved = sum(a.size * a.dtype.itemsize for a in arrays)
    if not early:
        flops, moved = 1, 1
    return pl.CostEstimate(flops=flops, bytes_accessed=moved, transcendentals=0)


def params():
    return pltpu.CompilerParams(vmem_limit_bytes=vmem_bytes)


def shape_of(shape, dtype):
    return jax.ShapeDtypeStruct(shape, dtype)


message_rows = 144
sizes = (128, 128, 64, 64, 128) * 2


def q_specs(q_refs, chunk):
    return [
        pl.BlockSpec((size, chunk), lambda k: (0, k)) for size, q in zip(sizes, q_refs)
    ]


def hard_kernel(bases, *rest):
    infos, rest = rest[:8], rest[8:]
    q_refs = rest[:10]
    n1, n2, e1, e2, row_sum, s1, s2, codes, acc1, acc2, sq1, sq2 = rest[10:]
    k = pl.program_id(0)

    @pl.when(k == 0)
    def _():
        for ref in (acc1, acc2, sq1, sq2):
            ref[...] = jnp.zeros_like(ref)

    q_all = stacked(q_refs)
    for n, acc, sq in ((n1[...], acc1, sq1), (n2[...], acc2, sq2)):
        acc[...] += dot_nt(n, q_all)
        sq[...] += lane_squares(n)

    @pl.when(k == pl.num_programs(0) - 1)
    def _():
        for slot in range(8):
            info = infos[slot][...].astype(f32)
            code = info[0:8, 0:128] * 256.0 + info[8:16, 0:128]
            q_scale = info[0:1, 128:256] + info[1:2, 128:256] + info[2:3, 128:256]
            codes[slot] = jnp.concatenate([code[0:7], q_scale], axis=0)
        sums = [jnp.zeros((1, 128), f32) for _ in range(8)]
        for h, (acc, sq, e, s) in enumerate(((acc1, sq1, e1, s1), (acc2, sq2, e2, s2))):
            scale = inverse_norm(sq[...])
            s[...] = jnp.broadcast_to(scale, s.shape)
            rows = lax.broadcasted_iota(jnp.int32, (acc.shape[0], 128), 0).astype(f32) + bases[h]
            for slot in range(8):
                lanes = slice(slot * 128, slot * 128 + 128)
                score = acc[:, lanes] * (scale * inv_temp) * codes[slot, 7:8, :]
                hits = jnp.zeros(rows.shape, f32)
                for which in range(7):
                    hits += jnp.where(rows == codes[slot, which : which + 1, :], 1.0, 0.0)
                weight = hits * jnp.exp(score)
                e[:, lanes] = weight
                sums[slot] += jnp.sum(weight, axis=0, keepdims=True)
        for slot in range(8):
            row_sum[slot : slot + 1, :] = sums[slot]


def hard_scores(bases, q_refs, n1, n2, chunk=1024):
    rows, width = n1.shape
    tails = [q for q in q_refs if q.shape[0] % 128 == 16 or q.shape[0] % 64 == 16]
    outs = (
        shape_of((rows, 1024), f32),
        shape_of((rows, 1024), f32),
        shape_of((8, 128), f32),
        shape_of((rows, 128), f32),
        shape_of((rows, 128), f32),
        shape_of((8, 8, 128), f32),
    )
    return pl.pallas_call(
        hard_kernel,
        grid=(width // chunk,),
        in_specs=[smem_spec()]
        + [pl.BlockSpec((16, 256), lambda k, at=x.shape[0] // 16 - 1: (at, 0)) for x in tails]
        + q_specs(q_refs, chunk)
        + [cols_spec(x, chunk) for x in (n1, *n2)],
        out_specs=[whole_spec(o) for o in outs],
        out_shape=outs,
        scratch_shapes=[pltpu.VMEM((rows, 1024), f32)] * 2 + [pltpu.VMEM((rows, 128), f32)] * 2,
        compiler_params=params(),
        cost_estimate=cost(4 * rows * 1024 * width, n1, *n2, *q_refs, *outs[:2]),
        name="hard_scores",
    )(bases, *tails, *q_refs, n1, *n2)


def hot(start, count, pos):
    rows = lax.broadcasted_iota(jnp.int32, (count, pos.shape[1]), 0) + start
    return jnp.where(rows.astype(f32) == pos, 1.0, 0.0)


def hot_all(places, pos):
    return jnp.concatenate([hot(places[block], 64, pos) for block in range(8)], axis=0)


def batch_kernel(places, about, sums, p_all, *rest):
    q_refs = rest[:-6]
    e, total, stats, scales, acc, sq = rest[-6:]
    k = pl.program_id(0)

    @pl.when(k == 0)
    def _():
        acc[...] = jnp.zeros_like(acc)
        sq[...] = jnp.zeros_like(sq)

    acc[...] += dot_nt(p_all[...], stacked(q_refs))
    sq[...] += lane_squares(p_all[...])

    @pl.when(k == pl.num_programs(0) - 1)
    def _():
        scale = inverse_norm(sq[...])
        scales[...] = jnp.broadcast_to(scale, scales.shape)
        score = acc[...] * (scale * inv_temp) * about[0:1, :]
        weight = jnp.exp(score)
        e[...] = weight
        total[0:1, :] = sums[0:1, :] + jnp.sum(weight, axis=0, keepdims=True)
        total[1:8, :] = sums[1:8, :]
        chosen = score * hot_all(places, about[1:2, :])
        stats[...] = jnp.broadcast_to(jnp.sum(chosen, axis=0, keepdims=True), stats.shape)


def batch_scores(places, about, sums, p_all, q_refs):
    rows, width = p_all.shape
    outs = (
        shape_of((rows, 128), f32),
        shape_of((8, 128), f32),
        shape_of((8, 128), f32),
        shape_of((rows, 128), f32),
    )
    return pl.pallas_call(
        batch_kernel,
        grid=(width // 2048,),
        in_specs=[smem_spec(), whole_spec(about), whole_spec(sums)]
        + [cols_spec(x) for x in (p_all, *q_refs)],
        out_specs=[whole_spec(o) for o in outs],
        out_shape=outs,
        scratch_shapes=[pltpu.VMEM((rows, 128), f32), pltpu.VMEM((rows, 128), f32)],
        compiler_params=params(),
        cost_estimate=cost(2 * rows * 128 * width, p_all, *q_refs, *outs),
        name="batch_scores",
    )(places, about, sums, p_all, *q_refs)


def back_kernel(first, e1, e2, s1, s2, n1, n2, *rest):
    turned = rest[-1]

    @pl.when(pl.program_id(0) == 0)
    def _():
        rows = e1.shape[0]
        turned[:, :rows] = jnp.transpose(e1[...] * s1[:, 0:1]).astype(bf16)
        turned[:, rows:] = jnp.transpose(e2[...] * s2[:, 0:1]).astype(bf16)

    part = dot_nn(turned[...], stacked([n1, n2]))
    if first:
        rest[0][...] = part.astype(bf16)
    else:
        got, home, u1, u2, u3 = rest[:5]
        part = part + got[...].astype(f32)
        home[...] = part[:128]
        for at, ref in enumerate((u1, u2, u3)):
            ref[...] = part[128 + at * 128 : 256 + at * 128].astype(bf16)


def hard_back(half, e1, e2, s1, s2, n1, n2, got=None):
    rows, width = n1.shape
    first = got is None
    if first:
        outs = (shape_of((512, width), bf16),)
        extra = ()
    else:
        outs = (shape_of((128, width), f32),) + (shape_of((128, width), bf16),) * 3
        extra = (got,)
    e_spec = pl.BlockSpec((rows, 512), lambda k: (0, half))
    return pl.pallas_call(
        functools.partial(back_kernel, first),
        grid=(width // 2048,),
        in_specs=[e_spec, e_spec, whole_spec(s1), whole_spec(s2)]
        + [cols_spec(x) for x in (n1, *n2, *extra)],
        out_specs=[cols_spec(o) for o in outs],
        out_shape=outs,
        scratch_shapes=[pltpu.VMEM((512, 2 * rows), bf16)],
        compiler_params=params(),
        cost_estimate=cost(2 * 512 * 2 * rows * width, n1, *n2, e1, *outs),
        name="hard_back",
    )(e1, e2, s1, s2, n1, *n2, *extra)


def pool_kernel(e, fac, *rest):
    q_refs = rest[:10]
    out, coef = rest[10:]

    @pl.when(pl.program_id(0) == 0)
    def _():
        for slot in range(8):
            lanes = slice(slot * 128, slot * 128 + 128)
            coef[:, lanes] = (e[:, lanes] * fac[slot : slot + 1, :]).astype(bf16)

    out[...] = dot_nn(coef[...], stacked(q_refs)).astype(out.dtype)


def pool_part(e, fac, q_refs, dtype):
    rows = e.shape[0]
    width = q_refs[0].shape[1]
    out = shape_of((rows, width), dtype)
    return pl.pallas_call(
        pool_kernel,
        grid=(width // 2048,),
        in_specs=[whole_spec(e), whole_spec(fac)] + q_specs(q_refs, 2048),
        out_specs=cols_spec(out),
        out_shape=out,
        scratch_shapes=[pltpu.VMEM((rows, 1024), bf16)],
        compiler_params=params(),
        cost_estimate=cost(2 * rows * 1024 * width, e, out, *q_refs),
        name="pool_part",
    )(e, fac, *q_refs)


def query_kernel(places, about, e, scales, p_all, out, turned):
    @pl.when(pl.program_id(0) == 0)
    def _():
        target = hot_all(places, about[2:3, :])
        coef = (e[...] * about[0:1, :] - about[1:2, :] * target) * scales[:, 0:1]
        turned[...] = jnp.transpose(coef).astype(bf16)

    out[...] = dot_nn(turned[...], p_all[...])


def query_part(places, about, e, scales, p_all):
    rows, width = p_all.shape
    out = shape_of((128, width), f32)
    return pl.pallas_call(
        query_kernel,
        grid=(width // 2048,),
        in_specs=[smem_spec()] + [whole_spec(x) for x in (about, e, scales)] + [cols_spec(p_all)],
        out_specs=cols_spec(out),
        out_shape=out,
        scratch_shapes=[pltpu.VMEM((128, rows), bf16)],
        compiler_params=params(),
        cost_estimate=cost(2 * rows * 128 * width, out, p_all),
        name="query_part",
    )(places, about, e, scales, p_all)


def passage_kernel(turns, places, about_a, about_b, e_a, e_b, *rest):
    home, d1, d2, d3, coef = rest[-5:]
    q_refs = rest[:-5]

    @pl.when(pl.program_id(0) == 0)
    def _():
        for at, (about, e) in enumerate(((about_a, e_a), (about_b, e_b))):
            lanes = slice(at * 128, at * 128 + 128)
            for block in range(4):
                start = pl.multiple_of(turns[block] * 128, 128)
                target = hot(places[2 * turns[block]], 64, about[2:3, :])
                part = e[pl.ds(start, 64), :] * about[0:1, :] - about[1:2, :] * target
                coef[block * 64 : block * 64 + 64, lanes] = (part * about[3:4, :]).astype(bf16)

    part = dot_nn(coef[...], stacked(q_refs))
    home[...] = part[:64]
    for at, ref in enumerate((d1, d2, d3)):
        ref[...] = part[64 + at * 64 : 128 + at * 64].astype(bf16)


def passage_part(turns, places, about_a, about_b, e_a, e_b, q_refs):
    width = q_refs[0].shape[1]
    outs = (shape_of((64, width), f32),) + (shape_of((64, width), bf16),) * 3
    return pl.pallas_call(
        passage_kernel,
        grid=(width // 2048,),
        in_specs=[smem_spec(), smem_spec()]
        + [whole_spec(x) for x in (about_a, about_b, e_a, e_b)]
        + [cols_spec(x) for x in q_refs],
        out_specs=[cols_spec(o) for o in outs],
        out_shape=outs,
        scratch_shapes=[pltpu.VMEM((256, 256), bf16)],
        compiler_params=params(),
        cost_estimate=cost(2 * 256 * 256 * width, *q_refs, *outs),
        name="passage_part",
    )(turns, places, about_a, about_b, e_a, e_b, *q_refs)


def last_kernel(n_parts, has_fac, *refs):
    parts = refs[:n_parts]
    rest = list(refs[n_parts:])
    total = None
    for ref in parts:
        pieces = [ref[...]] if len(ref.shape) == 2 else [ref[i] for i in range(ref.shape[0])]
        for piece in pieces:
            piece = piece.astype(f32)
            total = piece if total is None else total + piece
    if has_fac:
        fac, plain = rest[0], rest[1]
        total = total * fac[:, 0:1] + plain[...]
        rest = rest[2:]
    raw, out = rest[0], rest[-1]
    rows = raw[...].astype(f32)
    scale = lax.rsqrt(jnp.sum(rows * rows, axis=1, keepdims=True) + eps)
    along = jnp.sum(rows * total, axis=1, keepdims=True) * (scale * scale)
    out[...] = (total - rows * along) * (scale * inv_temp)


def last_step(parts, raw, fac=None, plain=None, step=step_rows):
    width = raw.shape[1]
    rows = raw.shape[0]

    def spec(x):
        if len(x.shape) == 3:
            return pl.BlockSpec((x.shape[0], step, x.shape[2]), lambda i: (0, i, 0))
        return pl.BlockSpec((step, x.shape[1]), lambda i: (i, 0))

    extra = () if fac is None else (fac, plain)
    ins = (*parts, *extra, raw)
    out = shape_of(raw.shape, f32)
    return pl.pallas_call(
        functools.partial(last_kernel, len(parts), fac is not None),
        grid=(rows // step,),
        in_specs=[spec(x) for x in ins],
        out_specs=spec(out),
        out_shape=out,
        compiler_params=params(),
        cost_estimate=cost(8 * rows * width, out, *ins),
        name="last_step",
    )(*ins)


def local(queries, passages, pool, query_count, positive, neg_owner, neg_row):
    n_query = queries.shape[0]
    n_pool = pool.shape[0]
    grp = lax.axis_index("grp")
    loop = lax.axis_index("loop")
    zi, xh, ci = grp // 4, (grp // 2) % 2, grp % 2
    xl, yi = loop // 4, loop % 4

    valid = (lax.iota(jnp.int32, n_query) < query_count.reshape(())).astype(f32)
    wide = queries.astype(f32)
    q_scale = lax.rsqrt(jnp.sum(wide * wide, axis=1) + eps)
    high = lax.reduce_precision(q_scale, 8, 7)
    mid = lax.reduce_precision(q_scale - high, 8, 7)
    low = q_scale - high - mid
    zero_row = jnp.zeros((1, n_query), f32)
    owners = jnp.where(valid[None, :] > 0, neg_owner.T.astype(f32), -1.0)
    left = jnp.concatenate([owners, zero_row, neg_row.T.astype(f32), zero_row], axis=0)
    right = jnp.concatenate([high[None], mid[None], low[None], jnp.tile(zero_row, (13, 1))], axis=0)
    info = jnp.concatenate([left, right], axis=1).astype(bf16)
    info = jnp.pad(info, ((0, 0), (0, queries.shape[1] - 2 * n_query)))
    message = jnp.concatenate([queries, info], axis=0)

    px = hop_xl(passages)
    q1 = hop_z(message, -1)
    q3 = hop_z(message, 1)
    pool_late, px_late, passages_late = after((pool, px, passages), px, message)
    pool_x = (hop_xh(pool_late),)
    pc = jnp.concatenate([passages_late, px_late], axis=0)
    y_groups = [[l * 4 + y for y in range(4)] for l in range(2)]
    p_all = lax.all_gather(pc, "loop", axis=0, tiled=True, axis_index_groups=y_groups)
    side0 = hop_core(message)
    q2a = hop_z(q1[:64], -1)
    q2b = hop_z(q3[64:], 1)
    q1_late, q3_late = after((q1, q3), q2a, q2b)
    side1, side3 = hop_core(q1_late), hop_core(q3_late)
    side2a, side2b = hop_core(q2a), hop_core(q2b)
    q_refs = (message, q1, q2a, q2b, q3, side0, side1, side2a, side2b, side3)
    bases = jnp.stack([grp * n_pool, (grp ^ 2) * n_pool]).astype(f32)
    steps = jnp.arange(4, dtype=jnp.int32)
    turns = (yi + steps) % 4
    places = jnp.stack([xl * 4 + steps, (1 - xl) * 4 + steps], axis=1).reshape(8) * passages.shape[0]
    pos = positive.astype(f32)
    about_first = jnp.concatenate([q_scale[None], pos[None], jnp.tile(zero_row, (6, 1))], axis=0)

    e1, e2, hard_sums, s1, s2, codes = hard_scores(bases, q_refs, pool, pool_x)
    q_late, about_late = after((queries, about_first), pool_x[0])
    q_xa = hop_xl(q_late[:64])
    about_first_x = hop_xl(about_late)
    (e1_side,) = after((e1,), q_xa, about_first_x)
    (q_later,) = after((queries,), q_xa)
    q_xb = hop_xl(q_later[64:])
    (u_side,) = hard_back(1, e1_side, e2, s1, s2, pool, pool_x)
    u_got = hop_core(u_side)
    (hard_sums,) = after((hard_sums,), u_side)
    e_batch, part, chosen, p_scales = batch_scores(places, about_first, hard_sums, p_all, (queries,))

    got = [hop_z(part, -by) for by in (1, 2, 3)]
    got, _ = lax.optimization_barrier((got, u_side))
    total = part.reshape(2, 4, n_query)
    for by in (1, 2, 3):
        total = total + jnp.roll(got[by - 1].reshape(2, 4, n_query), by, axis=1)
    core_total = hop_core(total)
    total = total + core_total[::-1]
    live = (codes[:, 0, :] >= 0).astype(f32)
    fac = live * codes[:, 7, :] / total.reshape(8, n_query)
    own_total = total[0, 0]
    loss = valid * (jnp.log(own_total) - chosen[0])
    own_fac = valid / own_total
    about = jnp.concatenate(
        [own_fac[None], valid[None], pos[None], q_scale[None], jnp.tile(zero_row, (4, 1))], axis=0
    )
    about_x = hop_xl(about)

    dn_far = pool_part(e2, fac, q_refs, bf16)
    dn_far, _ = lax.optimization_barrier((dn_far, (about_x, q_xb)))
    dn_x = hop_xh(dn_far)
    (u_got,) = after((u_got,), dn_far)
    u_home, u1, u2, u3 = hard_back(0, e1, e2, s1, s2, pool, pool_x, u_got)
    u_parts = (u_home, hop_z(u1, 1), hop_z(u2, 2), hop_z(u3, -1))
    q_xa, q_xb = after((q_xa, q_xb), u_home)
    e_batch_x, _, _, _ = batch_scores(places, about_first_x, hard_sums, p_all, (q_xa, q_xb))
    d_home, d1, d2, d3 = passage_part(
        turns, places, about, about_x, e_batch, e_batch_x, (queries, q_xa, q_xb)
    )
    (e1_late,) = after((e1,), d_home)
    dn_home = pool_part(e1_late, fac, q_refs, f32)
    (e_late,) = after((e_batch,), dn_home)
    dq_batch = query_part(places, about, e_late, p_scales, p_all)
    fac_rows = jnp.broadcast_to(own_fac[:, None], (n_query, 128))
    d_one = hop_y(d1, 1)
    grad_pool = last_step((dn_home, dn_x), pool)
    (d2, d3, dq_batch) = after((d2, d3, dq_batch), grad_pool)
    d_two = hop_y(d2, 2)
    d_three = hop_y(d3, -1)
    grad_query = last_step(u_parts, queries, fac_rows, dq_batch)
    (d_one, d_two, d_three), _ = lax.optimization_barrier(((d_one, d_two, d_three), grad_query))
    grad_passage = last_step((d_home, d_one, d_two, d_three), passages)
    return (loss, grad_query, grad_passage, grad_pool)


def solution(mesh):
    both = ("loop", "grp")
    return jax.shard_map(
        local,
        mesh=mesh,
        in_specs=(
            P(both, None),
            P(both, None),
            P(both, None),
            P("loop", "grp"),
            P(both),
            P(both, None),
            P(both, None),
        ),
        out_specs=(P(both), P(both, None), P(both, None), P(both, None)),
        check_vma=False,
    )
```

```python
import functools

import jax
import jax.numpy as jnp
from jax import lax
from jax.experimental import pallas as pl
from jax.experimental.pallas import tpu as pltpu
from jax.sharding import PartitionSpec as P

inv_temp = 50.0
eps = 1e-06
f32 = jnp.float32
bf16 = jnp.bfloat16
vmem_bytes = 56 << 20
step_rows = 64


def hop_z(x, by):
    return lax.ppermute(x, "grp", [(g, (g + 4 * by) % 16) for g in range(16)])


def hop_xh(x):
    return lax.ppermute(x, "grp", [(g, g ^ 2) for g in range(16)])


def hop_core(x):
    return lax.ppermute(x, "grp", [(g, g ^ 1) for g in range(16)])


def hop_xl(x):
    return lax.ppermute(x, "loop", [(l, l ^ 4) for l in range(8)])


def hop_y(x, by):
    return lax.ppermute(x, "loop", [(l, (l & 4) + (l + by) % 4) for l in range(8)])


def after(values, *first):
    got = lax.optimization_barrier((tuple(values), first))
    return got[0]


def dot_nt(a, b):
    return lax.dot_general(a, b, (((1,), (1,)), ((), ())), preferred_element_type=f32)


def dot_nn(a, b):
    return lax.dot_general(a, b, (((1,), (0,)), ((), ())), preferred_element_type=f32)


def lane_squares(block):
    wide = block.astype(f32)
    wide = wide * wide
    part = wide[:, :128]
    for at in range(128, wide.shape[1], 128):
        part = part + wide[:, at : at + 128]
    return part


def inverse_norm(part):
    return lax.rsqrt(jnp.sum(part, axis=1, keepdims=True) + eps)


def stacked(refs):
    parts = [r[...] for r in refs]
    return parts[0] if len(parts) == 1 else jnp.concatenate(parts, axis=0)


def cols_spec(x, chunk=2048):
    return pl.BlockSpec((x.shape[0], chunk), lambda k: (0, k))


def whole_spec(x):
    return pl.BlockSpec(x.shape, lambda k: (0,) * x.ndim)


def smem_spec():
    return pl.BlockSpec(memory_space=pltpu.SMEM)


def cost(flops, *arrays, early=False):
    moved = sum(a.size * a.dtype.itemsize for a in arrays)
    if not early:
        flops, moved = 1, 1
    return pl.CostEstimate(flops=flops, bytes_accessed=moved, transcendentals=0)


def params():
    return pltpu.CompilerParams(vmem_limit_bytes=vmem_bytes)


def shape_of(shape, dtype):
    return jax.ShapeDtypeStruct(shape, dtype)


message_rows = 144
sizes = (128, 128, 64, 64, 128) * 2


def q_specs(q_refs, chunk):
    return [
        pl.BlockSpec((size, chunk), lambda k: (0, k)) for size, q in zip(sizes, q_refs)
    ]


def hard_kernel(bases, before, *rest):
    infos, rest = rest[:8], rest[8:]
    q_refs = rest[:10]
    n1, n2, e1, e2, row_sum, s1, s2, codes, acc1, acc2, sq1, sq2 = rest[10:]
    k = pl.program_id(0)

    @pl.when(k == 0)
    def _():
        for ref in (acc1, acc2, sq1, sq2):
            ref[...] = jnp.zeros_like(ref)

    q_all = stacked(q_refs)
    for n, acc, sq in ((n1[...], acc1, sq1), (n2[...], acc2, sq2)):
        acc[...] += dot_nt(n, q_all)
        sq[...] += lane_squares(n)

    @pl.when(k == pl.num_programs(0) - 1)
    def _():
        for slot in range(8):
            info = infos[slot][...].astype(f32)
            code = info[0:8, 0:128] * 256.0 + info[8:16, 0:128]
            q_scale = info[0:1, 128:256] + info[1:2, 128:256] + info[2:3, 128:256]
            codes[slot] = jnp.concatenate([code[0:7], q_scale], axis=0)
        sums = [before[0:1, :]] + [jnp.zeros((1, 128), f32) for _ in range(7)]
        for h, (acc, sq, e, s) in enumerate(((acc1, sq1, e1, s1), (acc2, sq2, e2, s2))):
            scale = inverse_norm(sq[...])
            s[...] = jnp.broadcast_to(scale, s.shape)
            rows = lax.broadcasted_iota(jnp.int32, (acc.shape[0], 128), 0).astype(f32) + bases[h]
            for slot in range(8):
                lanes = slice(slot * 128, slot * 128 + 128)
                score = acc[:, lanes] * (scale * inv_temp) * codes[slot, 7:8, :]
                hits = jnp.zeros(rows.shape, f32)
                for which in range(7):
                    hits += jnp.where(rows == codes[slot, which : which + 1, :], 1.0, 0.0)
                weight = hits * jnp.exp(score)
                e[:, lanes] = weight
                sums[slot] += jnp.sum(weight, axis=0, keepdims=True)
        for slot in range(8):
            row_sum[slot : slot + 1, :] = sums[slot]


def hard_scores(bases, before, q_refs, n1, n2, chunk=1024):
    rows, width = n1.shape
    tails = [q for q in q_refs if q.shape[0] % 64 == 16]
    outs = (
        shape_of((rows, 1024), f32),
        shape_of((rows, 1024), f32),
        shape_of((8, 128), f32),
        shape_of((rows, 128), f32),
        shape_of((rows, 128), f32),
        shape_of((8, 8, 128), f32),
    )
    return pl.pallas_call(
        hard_kernel,
        grid=(width // chunk,),
        in_specs=[smem_spec(), whole_spec(before)]
        + [pl.BlockSpec((16, 256), lambda k, at=x.shape[0] // 16 - 1: (at, 0)) for x in tails]
        + q_specs(q_refs, chunk)
        + [cols_spec(x, chunk) for x in (n1, *n2)],
        out_specs=[whole_spec(o) for o in outs],
        out_shape=outs,
        scratch_shapes=[pltpu.VMEM((rows, 1024), f32)] * 2 + [pltpu.VMEM((rows, 128), f32)] * 2,
        compiler_params=params(),
        cost_estimate=cost(4 * rows * 1024 * width, n1, *n2, *q_refs, *outs[:2]),
        name="hard_scores",
    )(bases, before, *tails, *q_refs, n1, *n2)


def passage_rows(refs):
    pc, p1, p2, p2x, p3 = [r[...] for r in refs]
    near = [pc[:64], p1[:64], p2, p3[:64]]
    far = [pc[64:], p1[64:], p2x, p3[64:]]
    return jnp.concatenate(near + far, axis=0)


def hot(places, pos, block):
    rows = lax.broadcasted_iota(jnp.int32, (64, pos.shape[1]), 0).astype(f32)
    return jnp.where(rows + places[block] == pos, 1.0, 0.0)


def batch_kernel(places, about, *rest):
    p_refs = rest[:5]
    q_refs = rest[5:-5]
    e, stats, scales, acc, sq = rest[-5:]
    k = pl.program_id(0)

    @pl.when(k == 0)
    def _():
        acc[...] = jnp.zeros_like(acc)
        sq[...] = jnp.zeros_like(sq)

    p_all = passage_rows(p_refs)
    acc[...] += dot_nt(p_all, stacked(q_refs))
    sq[...] += lane_squares(p_all)

    @pl.when(k == pl.num_programs(0) - 1)
    def _():
        scale = inverse_norm(sq[...])
        scales[...] = jnp.broadcast_to(scale, scales.shape)
        score = acc[...] * (scale * inv_temp) * about[0:1, :]
        weight = jnp.exp(score)
        e[...] = weight
        chosen = jnp.zeros((1, 128), f32)
        for block in range(8):
            part = score[block * 64 : block * 64 + 64]
            chosen += jnp.sum(part * hot(places, about[1:2, :], block), axis=0, keepdims=True)
        stats[0:1, :] = jnp.sum(weight, axis=0, keepdims=True)
        stats[1:2, :] = chosen
        stats[2:8, :] = jnp.zeros((6, 128), f32)


def batch_scores(places, about, p_refs, q_refs):
    width = q_refs[0].shape[1]
    outs = (shape_of((512, 128), f32), shape_of((8, 128), f32), shape_of((512, 128), f32))
    return pl.pallas_call(
        batch_kernel,
        grid=(width // 2048,),
        in_specs=[smem_spec(), whole_spec(about)] + [cols_spec(x) for x in (*p_refs, *q_refs)],
        out_specs=[whole_spec(o) for o in outs],
        out_shape=outs,
        scratch_shapes=[pltpu.VMEM((512, 128), f32), pltpu.VMEM((512, 128), f32)],
        compiler_params=params(),
        cost_estimate=cost(2 * 512 * 128 * width, *q_refs, *p_refs, *outs),
        name="batch_scores",
    )(places, about, *p_refs, *q_refs)


def back_kernel(first, e1, e2, s1, s2, n1, n2, *rest):
    turned = rest[-1]

    @pl.when(pl.program_id(0) == 0)
    def _():
        rows = e1.shape[0]
        turned[:, :rows] = jnp.transpose(e1[...] * s1[:, 0:1]).astype(bf16)
        turned[:, rows:] = jnp.transpose(e2[...] * s2[:, 0:1]).astype(bf16)

    part = dot_nn(turned[...], stacked([n1, n2]))
    if first:
        rest[0][...] = part.astype(bf16)
    else:
        got, home, u1, u2, u3 = rest[:5]
        part = part + got[...].astype(f32)
        home[...] = part[:128]
        for at, ref in enumerate((u1, u2, u3)):
            ref[...] = part[128 + at * 128 : 256 + at * 128].astype(bf16)


def hard_back(half, e1, e2, s1, s2, n1, n2, got=None):
    rows, width = n1.shape
    first = got is None
    if first:
        outs = (shape_of((512, width), bf16),)
        extra = ()
    else:
        outs = (shape_of((128, width), f32),) + (shape_of((128, width), bf16),) * 3
        extra = (got,)
    e_spec = pl.BlockSpec((rows, 512), lambda k: (0, half))
    return pl.pallas_call(
        functools.partial(back_kernel, first),
        grid=(width // 2048,),
        in_specs=[e_spec, e_spec, whole_spec(s1), whole_spec(s2)]
        + [cols_spec(x) for x in (n1, *n2, *extra)],
        out_specs=[cols_spec(o) for o in outs],
        out_shape=outs,
        scratch_shapes=[pltpu.VMEM((512, 2 * rows), bf16)],
        compiler_params=params(),
        cost_estimate=cost(2 * 512 * 2 * rows * width, n1, *n2, e1, *outs),
        name="hard_back",
    )(e1, e2, s1, s2, n1, *n2, *extra)


def pool_kernel(e, fac, *rest):
    q_refs = rest[:10]
    out, coef = rest[10:]

    @pl.when(pl.program_id(0) == 0)
    def _():
        for slot in range(8):
            lanes = slice(slot * 128, slot * 128 + 128)
            coef[:, lanes] = (e[:, lanes] * fac[slot : slot + 1, :]).astype(bf16)

    out[...] = dot_nn(coef[...], stacked(q_refs)).astype(out.dtype)


def pool_part(e, fac, q_refs, dtype):
    rows = e.shape[0]
    width = q_refs[0].shape[1]
    out = shape_of((rows, width), dtype)
    return pl.pallas_call(
        pool_kernel,
        grid=(width // 2048,),
        in_specs=[whole_spec(e), whole_spec(fac)] + q_specs(q_refs, 2048),
        out_specs=cols_spec(out),
        out_shape=out,
        scratch_shapes=[pltpu.VMEM((rows, 1024), bf16)],
        compiler_params=params(),
        cost_estimate=cost(2 * rows * 1024 * width, e, out, *q_refs),
        name="pool_part",
    )(e, fac, *q_refs)


def query_kernel(places, about, e, scales, *rest):
    p_refs = rest[:5]
    out, turned = rest[5:]

    @pl.when(pl.program_id(0) == 0)
    def _():
        for block in range(8):
            rows = slice(block * 64, block * 64 + 64)
            coef = e[rows, :] * about[0:1, :] - about[1:2, :] * hot(places, about[2:3, :], block)
            turned[rows, :] = coef * scales[rows, 0:1]

    turn = jnp.transpose(turned[...]).astype(bf16)
    out[...] = dot_nn(turn, passage_rows(p_refs))


def query_part(places, about, e, scales, p_refs):
    width = p_refs[0].shape[1]
    out = shape_of((128, width), f32)
    return pl.pallas_call(
        query_kernel,
        grid=(width // 2048,),
        in_specs=[smem_spec(), whole_spec(about), whole_spec(e), whole_spec(scales)]
        + [cols_spec(p) for p in p_refs],
        out_specs=cols_spec(out),
        out_shape=out,
        scratch_shapes=[pltpu.VMEM((512, 128), f32)],
        compiler_params=params(),
        cost_estimate=cost(2 * 512 * 128 * width, out, *p_refs),
        name="query_part",
    )(places, about, e, scales, *p_refs)


def passage_kernel(places, about_a, about_b, e_a, e_b, q_a, q_b, q_c, home, d1, d2, d3, coef):
    @pl.when(pl.program_id(0) == 0)
    def _():
        for at, (about, e) in enumerate(((about_a, e_a), (about_b, e_b))):
            lanes = slice(at * 128, at * 128 + 128)
            for block in range(4):
                rows = slice(block * 64, block * 64 + 64)
                part = e[rows, :] * about[0:1, :] - about[1:2, :] * hot(places, about[2:3, :], block)
                coef[rows, lanes] = (part * about[3:4, :]).astype(bf16)

    part = dot_nn(coef[...], stacked([q_a, q_b, q_c]))
    home[...] = part[:64]
    for at, ref in enumerate((d1, d2, d3)):
        ref[...] = part[64 + at * 64 : 128 + at * 64].astype(bf16)


def passage_part(places, about_a, about_b, e_a, e_b, q_a, q_b):
    width = q_a.shape[1]
    outs = (shape_of((64, width), f32),) + (shape_of((64, width), bf16),) * 3
    near = pl.BlockSpec((256, 128), lambda k: (0, 0))
    return pl.pallas_call(
        passage_kernel,
        grid=(width // 2048,),
        in_specs=[smem_spec(), whole_spec(about_a), whole_spec(about_b), near, near]
        + [cols_spec(x) for x in (q_a, *q_b)],
        out_specs=[cols_spec(o) for o in outs],
        out_shape=outs,
        scratch_shapes=[pltpu.VMEM((256, 256), bf16)],
        compiler_params=params(),
        cost_estimate=cost(2 * 256 * 256 * width, q_a, *q_b, *outs),
        name="passage_part",
    )(places, about_a, about_b, e_a, e_b, q_a, *q_b)


def last_kernel(n_parts, has_fac, *refs):
    parts = refs[:n_parts]
    rest = list(refs[n_parts:])
    total = None
    for ref in parts:
        pieces = [ref[...]] if len(ref.shape) == 2 else [ref[i] for i in range(ref.shape[0])]
        for piece in pieces:
            piece = piece.astype(f32)
            total = piece if total is None else total + piece
    if has_fac:
        fac, plain = rest[0], rest[1]
        total = total * fac[:, 0:1] + plain[...]
        rest = rest[2:]
    raw, out = rest[0], rest[-1]
    rows = raw[...].astype(f32)
    scale = lax.rsqrt(jnp.sum(rows * rows, axis=1, keepdims=True) + eps)
    along = jnp.sum(rows * total, axis=1, keepdims=True) * (scale * scale)
    out[...] = (total - rows * along) * (scale * inv_temp)


def last_step(parts, raw, fac=None, plain=None, step=step_rows):
    width = raw.shape[1]
    rows = raw.shape[0]

    def spec(x):
        if len(x.shape) == 3:
            return pl.BlockSpec((x.shape[0], step, x.shape[2]), lambda i: (0, i, 0))
        return pl.BlockSpec((step, x.shape[1]), lambda i: (i, 0))

    extra = () if fac is None else (fac, plain)
    ins = (*parts, *extra, raw)
    out = shape_of(raw.shape, f32)
    return pl.pallas_call(
        functools.partial(last_kernel, len(parts), fac is not None),
        grid=(rows // step,),
        in_specs=[spec(x) for x in ins],
        out_specs=spec(out),
        out_shape=out,
        compiler_params=params(),
        cost_estimate=cost(8 * rows * width, out, *ins),
        name="last_step",
    )(*ins)


def local(queries, passages, pool, query_count, positive, neg_owner, neg_row):
    n_query = queries.shape[0]
    n_pool = pool.shape[0]
    grp = lax.axis_index("grp")
    loop = lax.axis_index("loop")
    zi, xh, ci = grp // 4, (grp // 2) % 2, grp % 2
    xl, yi = loop // 4, loop % 4

    valid = (lax.iota(jnp.int32, n_query) < query_count.reshape(())).astype(f32)
    wide = queries.astype(f32)
    q_scale = lax.rsqrt(jnp.sum(wide * wide, axis=1) + eps)
    high = lax.reduce_precision(q_scale, 8, 7)
    mid = lax.reduce_precision(q_scale - high, 8, 7)
    low = q_scale - high - mid
    zero_row = jnp.zeros((1, n_query), f32)
    owners = jnp.where(valid[None, :] > 0, neg_owner.T.astype(f32), -1.0)
    left = jnp.concatenate([owners, zero_row, neg_row.T.astype(f32), zero_row], axis=0)
    right = jnp.concatenate([high[None], mid[None], low[None], jnp.tile(zero_row, (13, 1))], axis=0)
    info = jnp.concatenate([left, right], axis=1).astype(bf16)
    info = jnp.pad(info, ((0, 0), (0, queries.shape[1] - 2 * n_query)))
    message = jnp.concatenate([queries, info], axis=0)

    px = hop_xl(passages)
    q1 = hop_z(message, -1)
    q3 = hop_z(message, 1)
    side0 = hop_core(message)
    pool_late, passages_late = after((pool, passages), px)
    pool_x = (hop_xh(pool_late),)
    pc = jnp.concatenate([passages_late, px], axis=0)
    p1 = hop_y(pc, -1)
    p3 = hop_y(pc, 1)
    q1_next, q3_next = after((q1, q3), pc)
    q2a = hop_z(q1_next[:64], -1)
    q2b = hop_z(q3_next[64:], 1)
    p2 = hop_y(p1[:64], -1)
    p2x = hop_y(p3[64:], 1)
    q1_late, q3_late = after((q1, q3), q2a, q2b)
    side1, side3 = hop_core(q1_late), hop_core(q3_late)
    side2a, side2b = hop_core(q2a), hop_core(q2b)
    q_refs = (message, q1, q2a, q2b, q3, side0, side1, side2a, side2b, side3)
    p_refs = (pc, p1, p2, p2x, p3)
    bases = jnp.stack([grp * n_pool, (grp ^ 2) * n_pool]).astype(f32)
    steps = jnp.arange(4, dtype=jnp.int32)
    y_places = (yi + steps) % 4
    places = (
        jnp.concatenate([xl * 4 + y_places, (1 - xl) * 4 + y_places]) * passages.shape[0]
    ).astype(f32)
    pos = positive.astype(f32)
    about_first = jnp.concatenate([q_scale[None], pos[None], jnp.tile(zero_row, (6, 1))], axis=0)

    e_batch, stats, p_scales = batch_scores(places, about_first, p_refs, (queries,))
    e1, e2, part, s1, s2, codes = hard_scores(bases, stats, q_refs, pool, pool_x)
    q_late, about_late = after((queries, about_first), pool_x[0])
    q_xa = hop_xl(q_late[:64])
    about_first_x = hop_xl(about_late)

    (e1_side, e2_side) = after((e1, e2), part, q_xa, about_first_x)
    (q_later,) = after((queries,), q_xa)
    q_xb = hop_xl(q_later[64:])
    got = [hop_z(part, -by) for by in (1, 2, 3)]
    (u_side,) = hard_back(1, e1_side, e2_side, s1, s2, pool, pool_x)
    u_got = hop_core(u_side)
    got, _ = lax.optimization_barrier((got, u_side))
    total = part.reshape(2, 4, n_query)
    for by in (1, 2, 3):
        total = total + jnp.roll(got[by - 1].reshape(2, 4, n_query), by, axis=1)
    core_total = hop_core(total)
    total = total + core_total[::-1]
    live = (codes[:, 0, :] >= 0).astype(f32)
    fac = live * codes[:, 7, :] / total.reshape(8, n_query)
    own_total = total[0, 0]
    loss = valid * (jnp.log(own_total) - stats[1])
    own_fac = valid / own_total
    about = jnp.concatenate(
        [own_fac[None], valid[None], pos[None], q_scale[None], jnp.tile(zero_row, (4, 1))], axis=0
    )
    about_x = hop_xl(about)

    dn_far = pool_part(e2, fac, q_refs, bf16)
    dn_far, _ = lax.optimization_barrier((dn_far, (about_x, q_xb)))
    dn_x = hop_xh(dn_far)
    (u_got,) = after((u_got,), dn_far)
    u_home, u1, u2, u3 = hard_back(0, e1, e2, s1, s2, pool, pool_x, u_got)
    u_parts = (u_home, hop_z(u1, 1), hop_z(u2, 2), hop_z(u3, -1))
    q_x = after((q_xa, q_xb), u_home)
    e_batch_x, _, _ = batch_scores(places, about_first_x, p_refs, q_x)
    d_home, d1, d2, d3 = passage_part(places, about, about_x, e_batch, e_batch_x, queries, q_x)
    (e1_late,) = after((e1,), d_home)
    dn_home = pool_part(e1_late, fac, q_refs, f32)
    (e_late,) = after((e_batch,), dn_home)
    dq_batch = query_part(places, about, e_late, p_scales, p_refs)
    (d2,) = after((d2,), dn_home)
    (d3,) = after((d3,), dq_batch)
    d_one, d_two, d_three = hop_y(d1, 1), hop_y(d2, 2), hop_y(d3, -1)
    fac_rows = jnp.broadcast_to(own_fac[:, None], (n_query, 128))
    grad_pool = last_step((dn_home, dn_x), pool)
    (dq_batch,) = after((dq_batch,), grad_pool)
    grad_query = last_step(u_parts, queries, fac_rows, dq_batch)
    (d_one, d_two, d_three), _ = lax.optimization_barrier(((d_one, d_two, d_three), grad_query))
    grad_passage = last_step((d_home, d_one, d_two, d_three), passages)
    return (loss, grad_query, grad_passage, grad_pool)


def solution(mesh):
    both = ("loop", "grp")
    return jax.shard_map(
        local,
        mesh=mesh,
        in_specs=(
            P(both, None),
            P(both, None),
            P(both, None),
            P("loop", "grp"),
            P(both),
            P(both, None),
            P(both, None),
        ),
        out_specs=(P(both), P(both, None), P(both, None), P(both, None)),
        check_vma=False,
    )
```
